256 devices in a mesh: row: 16 (over x_hi, z), blk: 16 (over x_lo, y, core).
Axes of the slice: x: 4 (x_hi: 2, x_lo: 2; x = x_hi * 2 + x_lo), y: 4, z: 8, core: 2. Of those that a mesh axis runs over, the one named last changes fastest.
Arguments:
- source_table: bfloat16 [8192, 512], P('blk'), may hold values from -6 to 6
- target_table: bfloat16 [131072, 512], P(('row', 'blk')), may hold values from -6 to 6
- message_weight: bfloat16 [512, 512], replicated, may hold values from -0.25 to 0.25
- self_weight: bfloat16 [512, 512], replicated, may hold values from -0.25 to 0.25
- tile_lists: int32 [256, 16], P(('row', 'blk')), may hold values from 0 to 15, each once within a row
- key_offsets: int32 [131072, 16], P(('row', 'blk')), may hold values from 0 to 511
- list_lengths: int32 [256], P(('row', 'blk')), may hold values from 1 to 16, 2048 in all
- cotangent: bfloat16 [131072, 512], P(('row', 'blk')), may hold values from -6 to 6
Outputs:
- updated: bfloat16 [131072, 512], P(('row', 'blk'))
- target_gradient: bfloat16 [131072, 512], P(('row', 'blk'))
- source_gradient: bfloat16 [8192, 512], P(('blk', 'row'))
- self_gradient: float32 [512, 512], replicated
- message_gradient: float32 [512, 512], replicated
The draws below stay inside these ranges and needn't reach their ends.
Inputs may be any that keep to these rules, and one draw needn't show every extreme that they name: Each row of tile_lists names every one of the 16 source tiles once. A target tile uses the first list_lengths entries of its row of tile_lists.
All inputs are finite; a program needn't handle non-finite values. No bound on the sum of `list_lengths` on one device may be relied on, other than what follows from the above.
Results may differ from the reference program's by a relative error of at most 0.0058.
Values may be sent and summed in bfloat16 or wider, within the bound.
A program may use at most 64 MiB of HBM per device.

```python
import math
import jax
import jax.numpy as jnp
import numpy as np
from jax import lax

HIDDEN_SIZE = 512
TILE = 512
TARGET_TILES = 256
SOURCE_TILES = 16
TARGET_ROWS = 131072
SOURCE_ROWS = 8192


def touch_ends(entries, key, smallest, top_value):
    place = [jax.random.randint(jax.random.fold_in(key, axis), (), 0, length) for axis, length in enumerate(entries.shape)]
    widest = entries.shape.index(max(entries.shape))
    neighbour = place[:widest] + [(place[widest] + 1) % entries.shape[widest]] + place[widest + 1:]
    return entries.at[tuple(place)].set(smallest).at[tuple(neighbour)].set(top_value)


def levels(stream_key, dims, pieces, least, top_value):
    loudness = 1.0
    for axis_at, shards_of in pieces:
        heights = jax.random.uniform(jax.random.fold_in(jax.random.fold_in(stream_key, 6), axis_at), (shards_of,), jnp.float32, least / len(pieces), top_value / len(pieces))
        loudness = loudness * jnp.repeat(jnp.exp(heights), dims[axis_at] // shards_of).reshape((-1,) + (1,) * (len(dims) - 1 - axis_at))
    return loudness


def split_up(count, total, most, skew):
    portions = [(1 << 20) // math.isqrt(rank ** skew) + 1 for rank in range(2, count + 1)]
    rest, holding = total - most - (count - 1), [1] * (count - 1)
    while rest > 0:
        free = [i for i in range(count - 1) if holding[i] < most]
        pool, left = sum([portions[i] for i in free]), rest
        for i in free:
            addition = min(most - holding[i], max(1, left * portions[i] // pool), rest)
            holding[i] = holding[i] + addition
            rest = rest - addition
    return np.array([most] + holding)


def ragged_sizes(key, amount, total, most, skew):
    if amount == 2:
        one = jax.random.randint(key, (), max(1, total - most), min(most, total - 1) + 1)
        return jnp.stack([one, total - one])
    lengths = jnp.asarray(split_up(amount, total, most, skew), jnp.int32)
    twos = (amount - 1) // 2
    giver, sink = lengths[1:1 + 2 * twos:2], lengths[2:2 + 2 * twos:2]
    room = jnp.minimum(giver - 1, most - sink)
    moved = jax.random.randint(jax.random.fold_in(key, 1), (twos,), 0, 1 << 20) % (room + 1)
    lengths = lengths.at[1:1 + 2 * twos:2].set(giver - moved).at[2:2 + 2 * twos:2].set(sink + moved)
    return lengths[jax.random.permutation(jax.random.fold_in(key, 2), amount)]


def noise(key, extent, scale, most, cuts=(), kind=jnp.bfloat16):
    array = scale * jax.random.normal(key, extent, jnp.float32)
    if cuts:
        array = array * levels(key, extent, cuts, -0.22, 0.18)
    return jnp.clip(array, -most, most).astype(kind)


def setup_inputs(seed: int = 0) -> dict:
    seeds = jax.random.split(jax.random.key(seed), 9)
    return {
        "source_table": noise(seeds[0], (SOURCE_ROWS, HIDDEN_SIZE), 1.0, 6.0, ((0, 16),)),
        "target_table": noise(seeds[1], (TARGET_ROWS, HIDDEN_SIZE), 1.0, 6.0, ((0, 256),)),
        "message_weight": noise(seeds[2], (HIDDEN_SIZE, HIDDEN_SIZE), HIDDEN_SIZE ** -0.5, 0.25),
        "self_weight": noise(seeds[3], (HIDDEN_SIZE, HIDDEN_SIZE), HIDDEN_SIZE ** -0.5, 0.25),
        "tile_lists": jax.vmap(lambda own: jax.random.permutation(own, SOURCE_TILES))(jax.random.split(seeds[4], TARGET_TILES)).reshape((TARGET_TILES, SOURCE_TILES)).astype(jnp.int32),
        "key_offsets": touch_ends(jax.random.randint(seeds[5], (TARGET_ROWS, SOURCE_TILES), 0, TILE), jax.random.fold_in(seeds[5], 1), 0, TILE - 1).astype(jnp.int32),
        "list_lengths": ragged_sizes(seeds[6], TARGET_TILES, TARGET_TILES * SOURCE_TILES // 2, SOURCE_TILES, 2).astype(jnp.int32),
        "cotangent": noise(seeds[7], (TARGET_ROWS, HIDDEN_SIZE), 1.0, 6.0, ((0, 256),)),
    }


def reference(source_table, target_table, message_weight, self_weight, tile_lists, key_offsets, list_lengths, cotangent):
    projected = jnp.dot(source_table, message_weight, preferred_element_type=jnp.float32).astype(jnp.bfloat16)
    row_tile = (jnp.arange(TARGET_ROWS) // TILE).astype(jnp.int32)
    row_length = list_lengths[row_tile]
    inverse = 1.0 / row_length.astype(jnp.float32)
    linked = (tile_lists[row_tile] * TILE + key_offsets).astype(jnp.int32)
    active = jnp.arange(SOURCE_TILES, dtype=jnp.int32)[None, :] < row_length[:, None]

    def gather_step(totals, inputs):
        index_col, active_col = inputs
        values = projected[index_col].astype(jnp.float32)
        return totals + jnp.where(active_col[:, None], values, jnp.float32(0.0)), None

    start_sum = jnp.zeros((TARGET_ROWS, HIDDEN_SIZE), jnp.float32)
    gathered, _ = lax.scan(gather_step, start_sum, (linked.T, active.T))
    gathered = gathered * inverse[:, None]
    preact = jnp.dot(target_table, self_weight, preferred_element_type=jnp.float32) + gathered
    sigmoid_pre = jax.nn.sigmoid(preact)
    updated = (target_table.astype(jnp.float32) + preact * sigmoid_pre).astype(jnp.bfloat16)
    upstream = cotangent.astype(jnp.float32)
    grad_pre = (upstream * sigmoid_pre * (1.0 + preact * (1.0 - sigmoid_pre))).astype(jnp.bfloat16)
    target_gradient = (upstream + jnp.dot(grad_pre, self_weight.T, preferred_element_type=jnp.float32)).astype(jnp.bfloat16)
    self_gradient = jnp.dot(target_table.T, grad_pre, preferred_element_type=jnp.float32) * (TARGET_ROWS ** -0.5)
    scaled = grad_pre.astype(jnp.float32) * inverse[:, None]

    def scatter_step(totals, inputs):
        index_col, active_col = inputs
        terms = jnp.where(active_col[:, None], scaled, jnp.float32(0.0))
        return totals + jax.ops.segment_sum(terms, index_col, num_segments=SOURCE_ROWS), None

    start_grad = jnp.zeros((SOURCE_ROWS, HIDDEN_SIZE), jnp.float32)
    source_sum, _ = lax.scan(scatter_step, start_grad, (linked.T, active.T))
    source_grad_rounded = source_sum.astype(jnp.bfloat16)
    source_gradient = jnp.dot(source_grad_rounded, message_weight.T, preferred_element_type=jnp.float32).astype(jnp.bfloat16)
    message_gradient = jnp.dot(source_table.T, source_grad_rounded, preferred_element_type=jnp.float32) * (SOURCE_ROWS ** -0.5)
    return updated, target_gradient, source_gradient, self_gradient, message_gradient
```

```python
import functools

import jax
import jax.numpy as jnp
from jax import lax
from jax.experimental import pallas as pl
from jax.experimental.pallas import tpu as pltpu
from jax.sharding import PartitionSpec as P

XN, YN, ZN = 4, 4, 8
HALF = 256
EXTRA = 16
F32 = jnp.float32
BF16 = jnp.bfloat16


def dot(a, b, ca=1, cb=0):
    return lax.dot_general(a, b, (((ca,), (cb,)), ((), ())), preferred_element_type=F32)


def slot(col, dy, core):
    return col * 8 + dy * 2 + core


def kernel(
    s_hbm, t_hbm, wm_hbm, ws_hbm, lists_ref, ko_ref, len_ref, cot_hbm,
    upd_hbm, tg_hbm, sg_ref, w_out,
    sbuf, gbuf, tv, cotv, wmv, wsv, acc, base, bbuf, updv, tgv, koff,
    give, got, wsend, wrecv, zbuf, wres, rsend, rrecv,
    lsem, ssend1, srecv1, ssend2, srecv2, gsem, wssem, wrsem, zssem, zrsem, assem, arsem, bssem, brsem, rssem, rrsem,
):
    r = lax.axis_index("row")
    b = lax.axis_index("blk")
    x = lax.div(r, 8) * 2 + lax.div(b, 8)
    y = lax.rem(lax.div(b, 2), 4)
    z = lax.rem(r, 8)
    c = lax.rem(b, 2)

    def dev(dx=0, dy=0, dz=0, flip=False):
        xx = lax.rem(x + dx, XN)
        yy = lax.rem(y + dy, YN)
        zz = lax.rem(z + dz, ZN)
        cc = 1 - c if flip else c
        return {"row": lax.div(xx, 2) * 8 + zz, "blk": lax.rem(xx, 2) * 8 + yy * 2 + cc}

    def remote(src, dst, ss, rs, to):
        return pltpu.make_async_remote_copy(
            src_ref=src, dst_ref=dst, send_sem=ss, recv_sem=rs,
            device_id=to, device_id_type=pl.DeviceIdType.MESH,
        )

    loads = {}
    for i, (name, src, dst) in enumerate((
        ("s", s_hbm, sbuf.at[0]), ("t", t_hbm, tv), ("ws", ws_hbm, wsv), ("wm", wm_hbm, wmv), ("cot", cot_hbm, cotv),
    )):
        loads[name] = pltpu.make_async_copy(src, dst, lsem.at[i])
        loads[name].start()

    plane = [(dx, dy) for dx in range(XN) for dy in range(YN) if (dx, dy) != (0, 0)]
    rows = [(dxh, dz) for dxh in range(2) for dz in range(ZN) if (dxh, dz) != (0, 0)]
    barrier = pltpu.get_barrier_semaphore()
    partners = [dev(flip=True)] + [dev(dx, dy) for dx, dy in plane] + [
        dev(2 * dxh, 0, dz) for dxh, dz in rows if (dxh, dz) != (1, 0)
    ]
    for to in partners:
        pl.semaphore_signal(barrier, inc=1, device_id=to, device_id_type=pl.DeviceIdType.MESH)
    pl.semaphore_wait(barrier, len(partners))

    sends = []

    class Gather:
        def __init__(self, buf, ssem, rsem):
            self.buf, self.ssem, self.rsem, self.n = buf, ssem, rsem, 0

        def send(self, t, h, to_t, to):
            cp = remote(
                self.buf.at[t, h], self.buf.at[to_t, h], self.ssem.at[self.n], self.rsem.at[to_t * 2 + h], to
            )
            cp.start()
            self.n += 1
            sends.append(cp)

        def start(self, h):
            t = slot(0, 0, 0)
            first = (1, 3) if h == 0 else (3, 1)
            for dy in first:
                self.send(t, h, slot(0, (4 - dy) % 4, 0), dev(0, dy))
            self.send(t, h, slot(1, 0, 0), dev(1 if h == 0 else 3, 0))
            self.send(t, h, slot(0, 0, 1), dev(flip=True))

        def wait(self, col, dy, core, h):
            t = slot(col, dy, core)
            remote(
                self.buf.at[t, h], self.buf.at[t, h], self.ssem.at[0], self.rsem.at[t * 2 + h], dev(flip=True)
            ).wait_recv()

        def take(self, col, dy, h):
            self.wait(col, dy, 0, h)
            t = slot(col, dy, 0)
            if col == 0:
                if (dy, h) == (3, 0):
                    self.send(t, h, slot(0, 2, 0), dev(0, 1))
                if (dy, h) == (1, 1):
                    self.send(t, h, slot(0, 2, 0), dev(0, 3))
                self.send(t, h, slot(1, dy, 0), dev(1 if h == 0 else 3, 0))
            self.send(t, h, slot(col, dy, 1), dev(flip=True))

    first = Gather(sbuf, ssend1, srecv1)
    loads["s"].wait()
    first.start(0)
    first.start(1)

    k_row = lax.broadcasted_iota(jnp.int32, (16, 16), 0)
    s_col = lax.broadcasted_iota(jnp.int32, (16, 16), 1)
    kc, kd, ke = k_row // 8, (k_row // 2) % 4, k_row % 2
    xl = lax.rem(x, 2)
    tile_id = ((xl + kc) % 2) * 8 + ((y + kd) % 4) * 2 + (c + ke) % 2
    pick = ((lists_ref[...] == tile_id) & (s_col < len_ref[...])).astype(F32).astype(BF16)
    keys = ko_ref[...] + 1
    k_hi = (keys // 256).astype(F32).astype(BF16)
    k_lo = (keys % 256).astype(F32).astype(BF16)
    koff[...] = dot(k_hi, pick, 1, 1) * 256.0 + dot(k_lo, pick, 1, 1) - 1.0
    length = len_ref[...].astype(F32)
    inverse = 1.0 / length
    hi_t = dot(pick, k_hi, 1, 1) + 4.0 * length
    lo_t = dot(pick, k_lo, 1, 1)
    for h in range(2):
        gbuf[0, h, HALF:, :HALF] = lo_t[:, h * HALF:(h + 1) * HALF].astype(BF16)
        gbuf[0, h, HALF:, HALF:] = hi_t[:, h * HALF:(h + 1) * HALF].astype(BF16)

    loads["t"].wait()
    loads["ws"].wait()
    base[...] = dot(tv[...], wsv[...])

    lanes = lax.broadcasted_iota(jnp.int32, (512, 512), 1).astype(F32)

    def gather_tile(t, init=False):
        pattern = jnp.where(koff[:, t:t + 1] == lanes, 1.0, 0.0).astype(BF16)
        added = dot(pattern, sbuf[t].reshape(512, 512))
        acc[...] = added if init else acc[...] + added

    gather_tile(slot(0, 0, 0), True)
    first.wait(0, 0, 1, 0)
    first.wait(0, 0, 1, 1)
    gather_tile(slot(0, 0, 1))
    first.take(0, 3, 0)
    first.take(0, 1, 1)
    first.take(1, 0, 0)
    first.take(1, 0, 1)
    gather_tile(slot(1, 0, 0))
    first.take(0, 1, 0)
    first.take(0, 3, 1)
    gather_tile(slot(0, 3, 0))
    gather_tile(slot(0, 1, 0))
    for dy, h in ((3, 0), (1, 1)):
        first.take(1, dy, h)
    first.take(0, 2, 0)
    first.take(0, 2, 1)
    gather_tile(slot(0, 2, 0))
    for col, dy in ((1, 0), (0, 3), (0, 1), (0, 2)):
        first.wait(col, dy, 1, 0)
        first.wait(col, dy, 1, 1)
        gather_tile(slot(col, dy, 1))
    first.take(1, 1, 0)
    first.take(1, 3, 1)
    gather_tile(slot(1, 1, 0))
    gather_tile(slot(1, 3, 0))
    first.take(1, 2, 0)
    first.take(1, 2, 1)
    for dy in (1, 3):
        first.wait(1, dy, 1, 0)
        first.wait(1, dy, 1, 1)
        gather_tile(slot(1, dy, 1))
    gather_tile(slot(1, 2, 0))
    first.wait(1, 2, 1, 0)
    first.wait(1, 2, 1, 1)
    gather_tile(slot(1, 2, 1))

    loads["wm"].wait()
    loads["cot"].wait()
    second = Gather(gbuf, ssend2, srecv2)
    for h in range(2):
        part = pl.ds(h * HALF, HALF)
        mean = (acc[part, :] * inverse).astype(BF16)
        bbuf[part, :] = mean
        pre = base[part, :] + dot(mean, wmv[...])
        sig = jax.nn.sigmoid(pre)
        grad = cotv[part, :].astype(F32) * sig * (1.0 + pre * (1.0 - sig))
        gbuf[0, h, :HALF, :] = grad.astype(BF16)
        second.start(h)
        updv[part, :] = (tv[part, :].astype(F32) + pre * sig).astype(BF16)
    out_u = pltpu.make_async_copy(updv, upd_hbm, lsem.at[5])
    out_u.start()

    grads = gbuf[0, :, :HALF, :].reshape(512, 512)
    is_self = c == 0
    t_val, b_val = tv[...], bbuf[...]
    give[...] = dot(jnp.where(is_self, b_val, t_val), grads, 0, 0).astype(BF16)
    to_sib = remote(give, got, gsem.at[0], gsem.at[1], dev(flip=True))
    to_sib.start()
    sends.append(to_sib)
    base[...] = dot(jnp.where(is_self, t_val, b_val), grads, 0, 0)
    tgv[...] = (cotv[...].astype(F32) + dot(grads, wsv[...], 1, 1)).astype(BF16)
    out_t = pltpu.make_async_copy(tgv, tg_hbm, lsem.at[6])
    out_t.start()

    to_sib.wait_recv()
    wsend[...] = (base[...] + got[...].astype(F32)).astype(BF16).reshape(16, 32, 512)
    place = x * 4 + y
    w_in = []
    for i, (dx, dy) in enumerate(plane):
        peer = lax.rem(x + dx, XN) * 4 + lax.rem(y + dy, YN)
        cp = remote(wsend.at[peer], wrecv.at[i], wssem.at[i], wrsem.at[i], dev(dx, dy))
        cp.start()
        w_in.append(cp)
        sends.append(cp)

    sub = lax.broadcasted_iota(jnp.int32, (512, HALF), 0).astype(F32)

    def scatter_half(col, dy, core, h, init=False):
        t = slot(col, dy, core)
        mine = slot(col, (4 - dy) % 4, core)
        notes = gbuf[t, h, HALF:, :].astype(F32)[mine:mine + 1, :]
        hi = notes[:, HALF:]
        count = jnp.floor(hi * 0.25)
        key = notes[:, :HALF] + (hi - 4.0 * count) * 256.0 - 1.0
        pattern = jnp.where(key == sub, 1.0, 0.0).astype(BF16)
        added = dot(pattern, gbuf[t, h, :HALF, :]) * (1.0 / count[:, :1])
        acc[...] = added if init else acc[...] + added

    scatter_half(0, 0, 0, 0, True)
    scatter_half(0, 0, 0, 1)
    for h in range(2):
        second.wait(0, 0, 1, h)
        scatter_half(0, 0, 1, h)

    second.take(0, 3, 0)
    second.take(0, 1, 1)
    second.take(1, 0, 0)
    second.take(1, 0, 1)
    scatter_half(1, 0, 0, 0)
    scatter_half(1, 0, 0, 1)
    second.take(0, 1, 0)
    second.take(0, 3, 1)

    total = wsend[place].astype(F32)
    for i, cp in enumerate(w_in):
        cp.wait_recv()
        total = total + wrecv[i].astype(F32)
    zbuf[z] = total.astype(BF16)
    z_in = []
    for dz in range(1, ZN):
        cp = remote(zbuf.at[z], zbuf.at[z], zssem.at[dz], zrsem.at[z], dev(0, 0, dz))
        cp.start()
        sends.append(cp)

    for h in range(2):
        scatter_half(0, 3, 0, h)
        scatter_half(0, 1, 0, h)
    for dy, h in ((3, 0), (1, 1)):
        second.take(1, dy, h)
        scatter_half(1, dy, 0, h)
    second.take(0, 2, 0)
    second.take(0, 2, 1)

    for dz in range(1, ZN):
        peer = lax.rem(z + dz, ZN)
        remote(zbuf.at[peer], zbuf.at[peer], zssem.at[dz], zrsem.at[peer], dev(flip=True)).wait_recv()
    total = zbuf[0].astype(F32)
    for i in range(1, ZN):
        total = total + zbuf[i].astype(F32)
    wres[c, place] = total.astype(BF16)
    for i, (dx, dy) in enumerate(plane):
        cp = remote(wres.at[c, place], wres.at[c, place], assem.at[i], arsem.at[i], dev(dx, dy))
        cp.start()
        sends.append(cp)

    for h in range(2):
        scatter_half(0, 2, 0, h)
    for col, dy in ((1, 0), (0, 3), (0, 1), (0, 2)):
        for h in range(2):
            second.wait(col, dy, 1, h)
            scatter_half(col, dy, 1, h)
    second.take(1, 1, 0)
    second.take(1, 3, 1)
    second.take(1, 2, 0)
    second.take(1, 2, 1)
    for dy, h in ((1, 0), (3, 1), (2, 0), (2, 1)):
        scatter_half(1, dy, 0, h)
    for dy in (1, 3, 2):
        for h in range(2):
            second.wait(1, dy, 1, h)
            scatter_half(1, dy, 1, h)

    rsend[...] = acc[...].astype(BF16).reshape(16, 32, 512)
    r_in = []
    for i, (dxh, dz) in enumerate(rows):
        peer = lax.rem(lax.div(r, 8) + dxh, 2) * 8 + lax.rem(z + dz, ZN)
        cp = remote(rsend.at[peer], rrecv.at[i], rssem.at[i], rrsem.at[i], dev(2 * dxh, 0, dz))
        cp.start()
        r_in.append(cp)
        sends.append(cp)

    for i, (dx, dy) in enumerate(plane):
        peer = lax.rem(x + (XN - dx), XN) * 4 + lax.rem(y + (YN - dy), YN)
        remote(wres.at[c, peer], wres.at[c, peer], assem.at[i], arsem.at[i], dev(flip=True)).wait_recv()
    cross = remote(wres.at[c], wres.at[c], bssem, brsem, dev(flip=True))
    cross.start()
    sends.append(cross)

    total = rsend[r].astype(F32)
    for i, cp in enumerate(r_in):
        cp.wait_recv()
        total = total + rrecv[i].astype(F32)
    sg_ref[...] = dot(total.astype(BF16), wmv[...], 1, 1).astype(BF16)

    remote(wres.at[1 - c], wres.at[1 - c], bssem, brsem, dev(flip=True)).wait_recv()
    out_w = pltpu.make_async_copy(wres, w_out, lsem.at[7])
    out_w.start()
    for cp in sends:
        cp.wait_send()
    out_u.wait()
    out_t.wait()
    out_w.wait()


def local(
    source_table, target_table, message_weight, self_weight, tile_lists, key_offsets, list_lengths, cotangent
):
    any_spec = pl.BlockSpec(memory_space=pl.ANY)
    vmem = pl.BlockSpec(memory_space=pltpu.VMEM)
    dma = pltpu.SemaphoreType.DMA
    square = (512, 512)
    updated, target_gradient, source_gradient, weights = pl.pallas_call(
        kernel,
        out_shape=(
            jax.ShapeDtypeStruct(square, BF16),
            jax.ShapeDtypeStruct(square, BF16),
            jax.ShapeDtypeStruct((32, 512), BF16),
            jax.ShapeDtypeStruct((2, 16, 32, 512), BF16),
        ),
        in_specs=[any_spec, any_spec, any_spec, any_spec, vmem, vmem, vmem, any_spec],
        out_specs=(any_spec, any_spec, vmem, any_spec),
        scratch_shapes=[
            pltpu.VMEM((16, 2, HALF, 512), BF16),
            pltpu.VMEM((16, 2, HALF + EXTRA, 512), BF16),
            pltpu.VMEM(square, BF16),
            pltpu.VMEM(square, BF16),
            pltpu.VMEM(square, BF16),
            pltpu.VMEM(square, BF16),
            pltpu.VMEM(square, F32),
            pltpu.VMEM(square, F32),
            pltpu.VMEM(square, BF16),
            pltpu.VMEM(square, BF16),
            pltpu.VMEM(square, BF16),
            pltpu.VMEM((512, 16), F32),
            pltpu.VMEM(square, BF16),
            pltpu.VMEM(square, BF16),
            pltpu.VMEM((16, 32, 512), BF16),
            pltpu.VMEM((15, 32, 512), BF16),
            pltpu.VMEM((8, 32, 512), BF16),
            pltpu.VMEM((2, 16, 32, 512), BF16),
            pltpu.VMEM((16, 32, 512), BF16),
            pltpu.VMEM((15, 32, 512), BF16),
            dma((8,)),
            dma((30,)), dma((32,)),
            dma((30,)), dma((32,)),
            dma((2,)),
            dma((15,)), dma((15,)),
            dma((8,)), dma((8,)),
            dma((15,)), dma((15,)),
            dma(()), dma(()),
            dma((15,)), dma((15,)),
        ],
        compiler_params=pltpu.CompilerParams(
            collective_id=0, has_side_effects=True, vmem_limit_bytes=56 * 1024 * 1024
        ),
    )(
        source_table.reshape(2, HALF, 512), target_table, message_weight, self_weight, tile_lists, key_offsets,
        list_lengths.reshape(1, 1), cotangent,
    )
    weights = weights.reshape(2, 512, 512).astype(F32)
    self_gradient = weights[0] * 131072 ** (-0.5)
    message_gradient = weights[1] * 8192 ** (-0.5)
    return updated, target_gradient, source_gradient, self_gradient, message_gradient


def solution(mesh):
    placed = (
        P("blk", None),
        P(("row", "blk"), None),
        P(),
        P(),
        P(("row", "blk"), None),
        P(("row", "blk"), None),
        P(("row", "blk")),
        P(("row", "blk"), None),
    )
    return jax.shard_map(
        local,
        mesh=mesh,
        in_specs=placed,
        out_specs=(
            P(("row", "blk"), None),
            P(("row", "blk"), None),
            P(("blk", "row"), None),
            P(),
            P(),
        ),
        check_vma=False,
    )
```

```python
import functools

import jax
import jax.numpy as jnp
from jax import lax
from jax.experimental import pallas as pl
from jax.experimental.pallas import tpu as pltpu
from jax.sharding import PartitionSpec as P

XN, YN, ZN = 4, 4, 8
HALF = 256
PIECES = 2
WIDE = 512 // PIECES
F32 = jnp.float32
BF16 = jnp.bfloat16


def dot(a, b, ca=1, cb=0):
    return lax.dot_general(a, b, (((ca,), (cb,)), ((), ())), preferred_element_type=F32)


def slot(col, dy, core):
    return col * 8 + dy * 2 + core


def kernel(
    s_hbm, t_hbm, wm_hbm, ws_hbm, lists_ref, ko_ref, len_ref, cot_hbm,
    upd_hbm, tg_hbm, sg_ref, w_out,
    sbuf, gbuf, notes, links, scale, tv, cotv, wmv, wsv, acc, base, bbuf, updv, tgv, koff, terms,
    give, got, wsend, wrecv, zbuf, wres, xsend, xrecv, dsend, drecv,
    lsem, ssend1, srecv1, nssem, nrsem, ssend2, srecv2, gsem, wssem, wrsem, zssem, zrsem, assem, arsem, bssem, brsem,
    xssem, xrsem, dssem, drsem,
):
    r = lax.axis_index("row")
    b = lax.axis_index("blk")
    x = lax.div(r, 8) * 2 + lax.div(b, 8)
    y = lax.rem(lax.div(b, 2), 4)
    z = lax.rem(r, 8)
    c = lax.rem(b, 2)

    def dev(dx=0, dy=0, dz=0, flip=False):
        xx = lax.rem(x + dx, XN)
        yy = lax.rem(y + dy, YN)
        zz = lax.rem(z + dz, ZN)
        cc = 1 - c if flip else c
        return {"row": lax.div(xx, 2) * 8 + zz, "blk": lax.rem(xx, 2) * 8 + yy * 2 + cc}

    def remote(src, dst, ss, rs, to):
        return pltpu.make_async_remote_copy(
            src_ref=src, dst_ref=dst, send_sem=ss, recv_sem=rs,
            device_id=to, device_id_type=pl.DeviceIdType.MESH,
        )

    loads = {}
    for i, (name, src, dst) in enumerate((
        ("s", s_hbm, sbuf.at[0]), ("t", t_hbm, tv), ("ws", ws_hbm, wsv), ("wm", wm_hbm, wmv), ("cot", cot_hbm, cotv),
    )):
        loads[name] = pltpu.make_async_copy(src, dst, lsem.at[i])
        loads[name].start()

    plane = [(dx, dy) for dx in range(XN) for dy in range(YN) if (dx, dy) != (0, 0)]
    barrier = pltpu.get_barrier_semaphore()
    partners = [dev(flip=True)] + [dev(dx, dy) for dx, dy in plane]
    partners += [dev(0, dy, flip=True) for dy in range(1, YN)] + [dev(dz=dz) for dz in range(1, ZN)]
    for to in partners:
        pl.semaphore_signal(barrier, inc=1, device_id=to, device_id_type=pl.DeviceIdType.MESH)
    pl.semaphore_wait(barrier, len(partners))

    sends = []

    class Gather:
        def __init__(self, buf, ssem, rsem):
            self.buf, self.ssem, self.rsem, self.n = buf, ssem, rsem, 0

        def send(self, t, h, to_t, to):
            cp = remote(
                self.buf.at[t, h], self.buf.at[to_t, h], self.ssem.at[self.n], self.rsem.at[to_t * 2 + h], to
            )
            cp.start()
            self.n += 1
            sends.append(cp)

        def start(self, h):
            t = slot(0, 0, 0)
            first = (1, 3) if h == 0 else (3, 1)
            for dy in first:
                self.send(t, h, slot(0, (4 - dy) % 4, 0), dev(0, dy))
            self.send(t, h, slot(1, 0, 0), dev(1 if h == 0 else 3, 0))
            self.send(t, h, slot(0, 0, 1), dev(flip=True))

        def wait(self, col, dy, core, h):
            t = slot(col, dy, core)
            remote(
                self.buf.at[t, h], self.buf.at[t, h], self.ssem.at[0], self.rsem.at[t * 2 + h], dev(flip=True)
            ).wait_recv()

        def take(self, col, dy, h):
            self.wait(col, dy, 0, h)
            t = slot(col, dy, 0)
            if col == 0:
                if (dy, h) == (3, 0):
                    self.send(t, h, slot(0, 2, 0), dev(0, 1))
                if (dy, h) == (1, 1):
                    self.send(t, h, slot(0, 2, 0), dev(0, 3))
                self.send(t, h, slot(1, dy, 0), dev(1 if h == 0 else 3, 0))
            self.send(t, h, slot(col, dy, 1), dev(flip=True))

    first = Gather(sbuf, ssend1, srecv1)
    loads["s"].wait()
    first.start(0)
    first.start(1)

    k_row = lax.broadcasted_iota(jnp.int32, (16, 16), 0)
    s_col = lax.broadcasted_iota(jnp.int32, (16, 16), 1)
    kc, kd, ke = k_row // 8, (k_row // 2) % 4, k_row % 2
    xl = lax.rem(x, 2)
    tile_id = ((xl + kc) % 2) * 8 + ((y + kd) % 4) * 2 + (c + ke) % 2
    pick = ((lists_ref[...] == tile_id) & (s_col < len_ref[...])).astype(F32).astype(BF16)
    keys = ko_ref[...] + 1
    k_hi = (keys // 256).astype(F32).astype(BF16)
    k_lo = (keys % 256).astype(F32).astype(BF16)
    koff[...] = dot(k_hi, pick, 0, 1) * 256.0 + dot(k_lo, pick, 0, 1) - 1.0
    length = len_ref[...].astype(F32)
    inverse = 1.0 / length
    notes[0, :16] = dot(pick, k_lo).astype(BF16)
    notes[0, 16:] = (dot(pick, k_hi) + 4.0 * length).astype(BF16)
    note_in = []
    for i, (dy, core) in enumerate([(dy, core) for dy in range(YN) for core in range(2) if (dy, core) != (0, 0)]):
        to = slot(0, (4 - dy) % 4, core)
        cp = remote(notes.at[0], notes.at[to], nssem.at[i], nrsem.at[to], dev(0, dy, flip=core == 1))
        cp.start()
        sends.append(cp)

    loads["t"].wait()
    loads["ws"].wait()
    base[...] = dot(tv[...], wsv[...])

    lanes = lax.broadcasted_iota(jnp.int32, (512, 512), 1).astype(F32)

    def gather_tile(t, init=False):
        pattern = jnp.where(koff[:, t:t + 1] == lanes, 1.0, 0.0).astype(BF16)
        added = dot(pattern, sbuf[t].reshape(512, 512))
        acc[...] = added if init else acc[...] + added

    sub = lax.broadcasted_iota(jnp.int32, (512, 512), 0).astype(F32)

    def link_tile(i):
        dy, core = i // 2, i % 2
        if i:
            remote(notes.at[i], notes.at[i], nssem.at[0], nrsem.at[i], dev(flip=True)).wait_recv()
        for col in range(2):
            k = slot(col, (4 - dy) % 4, core)
            hi = notes[i, 16:, :].astype(F32)[k:k + 1, :]
            count = jnp.floor(hi * 0.25)
            key = notes[i, :16, :].astype(F32)[k:k + 1, :] + (hi - 4.0 * count) * 256.0 - 1.0
            links[i, col * 512:(col + 1) * 512, :] = jnp.where(key == sub, 1.0, 0.0).astype(BF16)
        scale[i:i + 1, :] = 1.0 / count[:, :128]

    gather_tile(slot(0, 0, 0), True)
    link_tile(0)
    first.wait(0, 0, 1, 0)
    first.wait(0, 0, 1, 1)
    gather_tile(slot(0, 0, 1))
    first.take(0, 3, 0)
    first.take(0, 1, 1)
    first.take(1, 0, 0)
    first.take(1, 0, 1)
    gather_tile(slot(1, 0, 0))
    first.take(0, 1, 0)
    first.take(0, 3, 1)
    gather_tile(slot(0, 3, 0))
    gather_tile(slot(0, 1, 0))
    for i in range(1, 4):
        link_tile(i)
    for dy, h in ((3, 0), (1, 1)):
        first.take(1, dy, h)
    first.take(0, 2, 0)
    first.take(0, 2, 1)
    gather_tile(slot(0, 2, 0))
    for i in range(4, 8):
        link_tile(i)
    for col, dy in ((1, 0), (0, 3), (0, 1), (0, 2)):
        first.wait(col, dy, 1, 0)
        first.wait(col, dy, 1, 1)
        gather_tile(slot(col, dy, 1))
    first.take(1, 1, 0)
    first.take(1, 3, 1)
    gather_tile(slot(1, 1, 0))
    gather_tile(slot(1, 3, 0))
    first.take(1, 2, 0)
    first.take(1, 2, 1)
    for dy in (1, 3):
        first.wait(1, dy, 1, 0)
        first.wait(1, dy, 1, 1)
        gather_tile(slot(1, dy, 1))
    gather_tile(slot(1, 2, 0))
    first.wait(1, 2, 1, 0)
    first.wait(1, 2, 1, 1)
    gather_tile(slot(1, 2, 1))

    loads["wm"].wait()
    loads["cot"].wait()

    def ring(f, i, h, to_i, to, n):
        part = pl.ds(h * HALF, HALF)
        k = (f * 8 + to_i) * 2 + h
        cp = remote(gbuf.at[f, i, part], gbuf.at[f, to_i, part], ssend2.at[f * 14 + n], srecv2.at[k], to)
        cp.start()
        sends.append(cp)

    def arrive(f, i, h):
        part = pl.ds(h * HALF, HALF)
        remote(
            gbuf.at[f, i, part], gbuf.at[f, i, part], ssend2.at[0], srecv2.at[(f * 8 + i) * 2 + h], dev(flip=True)
        ).wait_recv()

    def own_out(f, h):
        for n, dy in enumerate((1, 3) if h == 0 else (3, 1)):
            ring(f, 0, h, (4 - dy) % 4 * 2, dev(0, dy), h * 3 + n)
        ring(f, 0, h, 1, dev(flip=True), h * 3 + 2)

    def take(f, dy, h):
        arrive(f, dy * 2, h)
        if (dy, h) == (3, 0):
            ring(f, dy * 2, h, 4, dev(0, 1), 6)
        if (dy, h) == (1, 1):
            ring(f, dy * 2, h, 4, dev(0, 3), 7)
        ring(f, dy * 2, h, dy * 2 + 1, dev(flip=True), 8 + (dy - 1) * 2 + h)

    for h in range(2):
        part = pl.ds(h * HALF, HALF)
        mean = (acc[part, :] * inverse).astype(BF16)
        bbuf[part, :] = mean
        pre = base[part, :] + dot(mean, wmv[...])
        sig = jax.nn.sigmoid(pre)
        grad = (cotv[part, :].astype(F32) * sig * (1.0 + pre * (1.0 - sig))).astype(BF16)
        for f in range(PIECES):
            gbuf[f, 0, part, :] = grad[:, f * WIDE:(f + 1) * WIDE]
        own_out(0, h)
        updv[part, :] = (tv[part, :].astype(F32) + pre * sig).astype(BF16)
    out_u = pltpu.make_async_copy(updv, upd_hbm, lsem.at[5])
    out_u.start()

    grads = jnp.concatenate([gbuf[f, 0] for f in range(PIECES)], axis=1)
    is_self = c == 0
    t_val, b_val = tv[...], bbuf[...]
    give[...] = dot(jnp.where(is_self, b_val, t_val), grads, 0, 0).astype(BF16)
    to_sib = remote(give, got, gsem.at[0], gsem.at[1], dev(flip=True))
    to_sib.start()
    sends.append(to_sib)
    base[...] = dot(jnp.where(is_self, t_val, b_val), grads, 0, 0)

    to_sib.wait_recv()
    wsend[...] = (base[...] + got[...].astype(F32)).astype(BF16).reshape(16, 32, 512)
    place = x * 4 + y
    w_in = []
    for i, (dx, dy) in enumerate(plane):
        peer = lax.rem(x + dx, XN) * 4 + lax.rem(y + dy, YN)
        cp = remote(wsend.at[peer], wrecv.at[i], wssem.at[i], wrsem.at[i], dev(dx, dy))
        cp.start()
        w_in.append(cp)
        sends.append(cp)

    tgv[...] = (cotv[...].astype(F32) + dot(grads, wsv[...], 1, 1)).astype(BF16)
    out_t = pltpu.make_async_copy(tgv, tg_hbm, lsem.at[6])
    out_t.start()

    def scatter(f, dy, core):
        i = dy * 2 + core
        added = dot(links[i], gbuf[f, i]) * scale[i:i + 1, :1]
        terms[f] = added if i == 0 else terms[f] + added

    def gather_piece(f):
        scatter(f, 0, 0)
        for h in range(2):
            arrive(f, 1, h)
        scatter(f, 0, 1)
        take(f, 3, 0)
        take(f, 1, 1)
        take(f, 3, 1)
        take(f, 1, 0)
        if f + 1 < PIECES:
            own_out(f + 1, 0)
            own_out(f + 1, 1)
        scatter(f, 3, 0)
        scatter(f, 1, 0)
        for i in (7, 3):
            for h in range(2):
                arrive(f, i, h)
            scatter(f, i // 2, 1)
        take(f, 2, 0)
        take(f, 2, 1)
        scatter(f, 2, 0)
        for h in range(2):
            arrive(f, 5, h)
        scatter(f, 2, 1)

    def x_out(f):
        xsend[f] = terms[f].astype(BF16).reshape(2, 2, HALF, WIDE)
        for dx in range(1, XN):
            xh = lax.div(lax.rem(x + dx, XN), 2)
            cp = remote(
                xsend.at[f, dx % 2, xh], xrecv.at[f, dx - 1], xssem.at[f * 3 + dx - 1], xrsem.at[f * 3 + dx - 1], dev(dx)
            )
            cp.start()
            sends.append(cp)

    def z_out(f):
        total = xsend[f, 0, lax.div(x, 2)].astype(F32)
        for i in range(XN - 1):
            remote(
                xrecv.at[f, i], xrecv.at[f, i], xssem.at[0], xrsem.at[f * 3 + i], dev(flip=True)
            ).wait_recv()
            total = total + xrecv[f, i].astype(F32)
        dsend[f] = total.astype(BF16).reshape(8, 32, WIDE)
        for dz in range(1, ZN):
            n = f * 7 + dz - 1
            cp = remote(
                dsend.at[f, lax.rem(z + dz, ZN)], drecv.at[f, dz - 1], dssem.at[n], drsem.at[n], dev(dz=dz)
            )
            cp.start()
            sends.append(cp)

    def finish(f):
        total = dsend[f, z].astype(F32)
        for i in range(ZN - 1):
            remote(
                drecv.at[f, i], drecv.at[f, i], dssem.at[0], drsem.at[f * 7 + i], dev(flip=True)
            ).wait_recv()
            total = total + drecv[f, i].astype(F32)
        return dot(total.astype(BF16), wmv[:, f * WIDE:(f + 1) * WIDE], 1, 1)

    def weights_z():
        total = wsend[place].astype(F32)
        for i, cp in enumerate(w_in):
            cp.wait_recv()
            total = total + wrecv[i].astype(F32)
        zbuf[z] = total.astype(BF16)
        for dz in range(1, ZN):
            cp = remote(zbuf.at[z], zbuf.at[z], zssem.at[dz], zrsem.at[z], dev(0, 0, dz))
            cp.start()
            sends.append(cp)

    def weights_out():
        for dz in range(1, ZN):
            peer = lax.rem(z + dz, ZN)
            remote(zbuf.at[peer], zbuf.at[peer], zssem.at[dz], zrsem.at[peer], dev(flip=True)).wait_recv()
        total = zbuf[0].astype(F32)
        for i in range(1, ZN):
            total = total + zbuf[i].astype(F32)
        wres[c, place] = total.astype(BF16)
        for i, (dx, dy) in enumerate(plane):
            cp = remote(wres.at[c, place], wres.at[c, place], assem.at[i], arsem.at[i], dev(dx, dy))
            cp.start()
            sends.append(cp)

    gather_piece(0)
    x_out(0)
    weights_z()
    for f in range(1, PIECES):
        gather_piece(f)
        x_out(f)
        z_out(f - 1)
        if f == 1:
            weights_out()
    out = finish(0)
    for f in range(1, PIECES - 1):
        out = out + finish(f)
    z_out(PIECES - 1)

    for i, (dx, dy) in enumerate(plane):
        peer = lax.rem(x + (XN - dx), XN) * 4 + lax.rem(y + (YN - dy), YN)
        remote(wres.at[c, peer], wres.at[c, peer], assem.at[i], arsem.at[i], dev(flip=True)).wait_recv()
    cross = remote(wres.at[c], wres.at[c], bssem, brsem, dev(flip=True))
    cross.start()
    sends.append(cross)

    sg_ref[...] = (out + finish(PIECES - 1)).astype(BF16)

    remote(wres.at[1 - c], wres.at[1 - c], bssem, brsem, dev(flip=True)).wait_recv()
    out_w = pltpu.make_async_copy(wres, w_out, lsem.at[7])
    out_w.start()
    for cp in sends:
        cp.wait_send()
    out_u.wait()
    out_t.wait()
    out_w.wait()


def place_outputs(upd, tg, sg, w, upd_out, tg_out, sg_out, self_out, message_out):
    upd_out[...] = upd[...]
    tg_out[...] = tg[...]
    sg_out[...] = sg[...]
    rows = w.shape[1] * 32
    self_out[...] = w[0].reshape(rows, 512).astype(F32) * 131072 ** (-0.5)
    message_out[...] = w[1].reshape(rows, 512).astype(F32) * 8192 ** (-0.5)


def local(
    source_table, target_table, message_weight, self_weight, tile_lists, key_offsets, list_lengths, cotangent
):
    any_spec = pl.BlockSpec(memory_space=pl.ANY)
    vmem = pl.BlockSpec(memory_space=pltpu.VMEM)
    dma = pltpu.SemaphoreType.DMA
    square = (512, 512)
    updated, target_gradient, source_gradient, weights = pl.pallas_call(
        kernel,
        out_shape=(
            jax.ShapeDtypeStruct(square, BF16),
            jax.ShapeDtypeStruct(square, BF16),
            jax.ShapeDtypeStruct((32, 512), BF16),
            jax.ShapeDtypeStruct((2, 16, 32, 512), BF16),
        ),
        in_specs=[any_spec, any_spec, any_spec, any_spec, vmem, vmem, vmem, any_spec],
        out_specs=(any_spec, any_spec, vmem, any_spec),
        scratch_shapes=[
            pltpu.VMEM((16, 2, HALF, 512), BF16),
            pltpu.VMEM((PIECES, 8, 512, WIDE), BF16),
            pltpu.VMEM((8, 32, 512), BF16),
            pltpu.VMEM((8, 1024, 512), BF16),
            pltpu.VMEM((8, 128), F32),
            pltpu.VMEM(square, BF16),
            pltpu.VMEM(square, BF16),
            pltpu.VMEM(square, BF16),
            pltpu.VMEM(square, BF16),
            pltpu.VMEM(square, F32),
            pltpu.VMEM(square, F32),
            pltpu.VMEM(square, BF16),
            pltpu.VMEM(square, BF16),
            pltpu.VMEM(square, BF16),
            pltpu.VMEM((512, 16), F32),
            pltpu.VMEM((PIECES, 1024, WIDE), F32),
            pltpu.VMEM(square, BF16),
            pltpu.VMEM(square, BF16),
            pltpu.VMEM((16, 32, 512), BF16),
            pltpu.VMEM((15, 32, 512), BF16),
            pltpu.VMEM((8, 32, 512), BF16),
            pltpu.VMEM((2, 16, 32, 512), BF16),
            pltpu.VMEM((PIECES, 2, 2, HALF, WIDE), BF16),
            pltpu.VMEM((PIECES, 3, HALF, WIDE), BF16),
            pltpu.VMEM((PIECES, 8, 32, WIDE), BF16),
            pltpu.VMEM((PIECES, 7, 32, WIDE), BF16),
            dma((8,)),
            dma((30,)), dma((32,)),
            dma((7,)), dma((8,)),
            dma((14 * PIECES,)), dma((16 * PIECES,)),
            dma((2,)),
            dma((15,)), dma((15,)),
            dma((8,)), dma((8,)),
            dma((15,)), dma((15,)),
            dma(()), dma(()),
            dma((3 * PIECES,)), dma((3 * PIECES,)),
            dma((7 * PIECES,)), dma((7 * PIECES,)),
        ],
        compiler_params=pltpu.CompilerParams(
            collective_id=0, has_side_effects=True, vmem_limit_bytes=56 * 1024 * 1024
        ),
    )(
        source_table.reshape(2, HALF, 512), target_table, message_weight, self_weight, tile_lists, key_offsets.T,
        list_lengths.reshape(1, 1), cotangent,
    )
    steps = 4
    rows = 512 // steps
    wide = pl.BlockSpec((rows, 512), lambda i: (i, 0))
    small = pl.BlockSpec((32, 512), lambda i: (0, 0))
    return pl.pallas_call(
        place_outputs,
        grid=(steps,),
        out_shape=(
            jax.ShapeDtypeStruct(square, BF16),
            jax.ShapeDtypeStruct(square, BF16),
            jax.ShapeDtypeStruct((32, 512), BF16),
            jax.ShapeDtypeStruct(square, F32),
            jax.ShapeDtypeStruct(square, F32),
        ),
        in_specs=[wide, wide, small, pl.BlockSpec((2, rows // 32, 32, 512), lambda i: (0, i, 0, 0))],
        out_specs=(wide, wide, small, wide, wide),
    )(updated, target_gradient, source_gradient, weights)


def solution(mesh):
    placed = (
        P("blk", None),
        P(("row", "blk"), None),
        P(),
        P(),
        P(("row", "blk"), None),
        P(("row", "blk"), None),
        P(("row", "blk")),
        P(("row", "blk"), None),
    )
    return jax.shard_map(
        local,
        mesh=mesh,
        in_specs=placed,
        out_specs=(
            P(("row", "blk"), None),
            P(("row", "blk"), None),
            P(("blk", "row"), None),
            P(),
            P(),
        ),
        check_vma=False,
    )
```

```python
import functools

import jax
import jax.numpy as jnp
from jax import lax
from jax.experimental import pallas as pl
from jax.experimental.pallas import tpu as pltpu
from jax.sharding import PartitionSpec as P

XN, YN, ZN = 4, 4, 8
HALF = 256
PIECES = 2
WIDE = 512 // PIECES
F32 = jnp.float32
BF16 = jnp.bfloat16


def dot(a, b, ca=1, cb=0):
    return lax.dot_general(a, b, (((ca,), (cb,)), ((), ())), preferred_element_type=F32)


def slot(col, dy, core):
    return col * 8 + dy * 2 + core


def kernel(
    s_hbm, t_hbm, wm_hbm, ws_hbm, lists_ref, ko_ref, len_ref, cot_hbm,
    upd_hbm, tg_hbm, sg_ref, w_out,
    sbuf, gbuf, notes, links, scale, tv, cotv, wmv, wsv, acc, base, bbuf, updv, tgv, koff, terms,
    give, got, wsend, wrecv, ysend, yrecv, zbuf, wres, xsend, xrecv, dsend, drecv,
    lsem, ssend1, srecv1, nssem, nrsem, ssend2, srecv2, gsem, wssem, wrsem, zssem, zrsem, assem, arsem, bssem, brsem,
    xssem, xrsem, dssem, drsem,
):
    r = lax.axis_index("row")
    b = lax.axis_index("blk")
    x = lax.div(r, 8) * 2 + lax.div(b, 8)
    y = lax.rem(lax.div(b, 2), 4)
    z = lax.rem(r, 8)
    c = lax.rem(b, 2)

    def dev(dx=0, dy=0, dz=0, flip=False):
        xx = lax.rem(x + dx, XN)
        yy = lax.rem(y + dy, YN)
        zz = lax.rem(z + dz, ZN)
        cc = 1 - c if flip else c
        return {"row": lax.div(xx, 2) * 8 + zz, "blk": lax.rem(xx, 2) * 8 + yy * 2 + cc}

    def remote(src, dst, ss, rs, to):
        return pltpu.make_async_remote_copy(
            src_ref=src, dst_ref=dst, send_sem=ss, recv_sem=rs,
            device_id=to, device_id_type=pl.DeviceIdType.MESH,
        )

    loads = {}
    for i, (name, src, dst) in enumerate((
        ("s", s_hbm, sbuf.at[0]), ("t", t_hbm, tv), ("ws", ws_hbm, wsv), ("wm", wm_hbm, wmv), ("cot", cot_hbm, cotv),
    )):
        loads[name] = pltpu.make_async_copy(src, dst, lsem.at[i])
        loads[name].start()

    plane = [(dx, dy) for dx in range(XN) for dy in range(YN) if (dx, dy) != (0, 0)]
    barrier = pltpu.get_barrier_semaphore()
    partners = [dev(flip=True)] + [dev(dx, dy) for dx, dy in plane]
    partners += [dev(0, dy, flip=True) for dy in range(1, YN)] + [dev(dz=dz) for dz in range(1, ZN)]
    for to in partners:
        pl.semaphore_signal(barrier, inc=1, device_id=to, device_id_type=pl.DeviceIdType.MESH)
    pl.semaphore_wait(barrier, len(partners))

    sends = []

    parity = lax.rem(z, 2)
    made = [0]

    def part_of(t, role):
        base_row = 2 * parity if role < 2 else 2 - 2 * parity
        return sbuf.at[t, base_row + role % 2]

    def push(t, role, to_t, to_role, to):
        cp = remote(part_of(t, role), part_of(to_t, role), ssend1.at[made[0]], srecv1.at[to_t * 4 + to_role], to)
        cp.start()
        made[0] += 1
        sends.append(cp)

    def got_part(col, dy, core, role):
        t = slot(col, dy, core)
        remote(part_of(t, role), part_of(t, role), ssend1.at[0], srecv1.at[t * 4 + role], dev(flip=True)).wait_recv()

    def got_tile(col, dy):
        for role in range(4):
            got_part(col, dy, 1, role)

    def fetch(col, dy, role):
        got_part(col, dy, 0, role)
        t = slot(col, dy, 0)
        if col == 0 and dy == 3 and role in (0, 2):
            push(t, role, slot(0, 2, 0), role, dev(0, 1))
        if col == 0 and dy == 1 and role in (1, 3):
            push(t, role, slot(0, 2, 0), role, dev(0, 3))
        if role < 2 and (col, dy) not in ((0, 2), (1, 0)):
            push(t, role, t, role + 2, dev(dz=ZN - 1 if role == 0 else 1))
        if role < 2 and col == 0:
            push(t, role, slot(1, dy, 0), role, dev(1 if role == 0 else 3))
        push(t, role, slot(col, dy, 1), role, dev(flip=True))

    loads["s"].wait()
    for role in (0, 1):
        push(0, role, slot(0, 3, 0), role, dev(0, 1))
        push(0, 1 - role, slot(0, 1, 0), 1 - role, dev(0, 3))
        push(0, 2 * role, slot(1, 0, 0), 2 * role, dev(1))
        push(0, 2 * role + 1, slot(1, 0, 0), 2 * role + 1, dev(3))
    for role in range(4):
        push(0, role, slot(0, 0, 1), role, dev(flip=True))

    k_row = lax.broadcasted_iota(jnp.int32, (16, 16), 0)
    s_col = lax.broadcasted_iota(jnp.int32, (16, 16), 1)
    kc, kd, ke = k_row // 8, (k_row // 2) % 4, k_row % 2
    xl = lax.rem(x, 2)
    tile_id = ((xl + kc) % 2) * 8 + ((y + kd) % 4) * 2 + (c + ke) % 2
    pick = ((lists_ref[...] == tile_id) & (s_col < len_ref[...])).astype(F32).astype(BF16)
    keys = ko_ref[...] + 1
    k_hi = (keys // 256).astype(F32).astype(BF16)
    k_lo = (keys % 256).astype(F32).astype(BF16)
    koff[...] = dot(k_hi, pick, 0, 1) * 256.0 + dot(k_lo, pick, 0, 1) - 1.0
    length = len_ref[...].astype(F32)
    inverse = 1.0 / length
    notes[0, :16] = dot(pick, k_lo).astype(BF16)
    notes[0, 16:] = (dot(pick, k_hi) + 4.0 * length).astype(BF16)
    note_in = []
    for i, (dy, core) in enumerate([(dy, core) for dy in range(YN) for core in range(2) if (dy, core) != (0, 0)]):
        to = slot(0, (4 - dy) % 4, core)
        cp = remote(notes.at[0], notes.at[to], nssem.at[i], nrsem.at[to], dev(0, dy, flip=core == 1))
        cp.start()
        sends.append(cp)

    loads["t"].wait()
    loads["ws"].wait()
    base[...] = dot(tv[...], wsv[...])

    lanes = lax.broadcasted_iota(jnp.int32, (512, 512), 1).astype(F32)

    def gather_tile(t, init=False):
        pattern = jnp.where(koff[:, t:t + 1] == lanes, 1.0, 0.0).astype(BF16)
        added = dot(pattern, sbuf[t].reshape(512, 512))
        acc[...] = added if init else acc[...] + added

    sub = lax.broadcasted_iota(jnp.int32, (512, 512), 0).astype(F32)

    def link_tile(i):
        dy, core = i // 2, i % 2
        if i:
            remote(notes.at[i], notes.at[i], nssem.at[0], nrsem.at[i], dev(flip=True)).wait_recv()
        for col in range(2):
            k = slot(col, (4 - dy) % 4, core)
            hi = notes[i, 16:, :].astype(F32)[k:k + 1, :]
            count = jnp.floor(hi * 0.25)
            key = notes[i, :16, :].astype(F32)[k:k + 1, :] + (hi - 4.0 * count) * 256.0 - 1.0
            links[i, col * 512:(col + 1) * 512, :] = jnp.where(key == sub, 1.0, 0.0).astype(BF16)
        scale[i:i + 1, :] = 1.0 / count[:, :128]

    gather_tile(slot(0, 0, 0), True)
    link_tile(0)
    fetch(0, 3, 0)
    fetch(0, 1, 1)
    fetch(1, 0, 0)
    fetch(1, 0, 1)
    got_tile(0, 0)
    gather_tile(slot(0, 0, 1))
    fetch(0, 3, 1)
    fetch(0, 1, 0)
    fetch(1, 0, 2)
    fetch(1, 0, 3)
    gather_tile(slot(1, 0, 0))
    fetch(0, 3, 2)
    fetch(0, 1, 3)
    fetch(0, 2, 0)
    fetch(0, 2, 1)
    fetch(1, 3, 0)
    fetch(1, 1, 1)
    link_tile(1)
    link_tile(2)
    fetch(0, 1, 2)
    fetch(0, 3, 3)
    gather_tile(slot(0, 1, 0))
    fetch(1, 1, 0)
    fetch(1, 3, 1)
    gather_tile(slot(0, 3, 0))
    fetch(0, 2, 2)
    fetch(0, 2, 3)
    fetch(1, 3, 2)
    fetch(1, 1, 3)
    gather_tile(slot(0, 2, 0))
    fetch(1, 2, 0)
    fetch(1, 2, 1)
    got_tile(1, 0)
    gather_tile(slot(1, 0, 1))
    fetch(1, 1, 2)
    fetch(1, 3, 3)
    for dy in (1, 3, 2):
        got_tile(0, dy)
        gather_tile(slot(0, dy, 1))
    gather_tile(slot(1, 1, 0))
    gather_tile(slot(1, 3, 0))
    for i in range(3, 8):
        link_tile(i)
    fetch(1, 2, 2)
    fetch(1, 2, 3)
    for dy in (1, 3):
        got_tile(1, dy)
        gather_tile(slot(1, dy, 1))
    gather_tile(slot(1, 2, 0))
    got_tile(1, 2)
    gather_tile(slot(1, 2, 1))

    loads["wm"].wait()
    loads["cot"].wait()

    def ring(f, i, h, to_i, to, n):
        part = pl.ds(h * HALF, HALF)
        k = (f * 8 + to_i) * 2 + h
        cp = remote(gbuf.at[f, i, part], gbuf.at[f, to_i, part], ssend2.at[f * 14 + n], srecv2.at[k], to)
        cp.start()
        sends.append(cp)

    def arrive(f, i, h):
        part = pl.ds(h * HALF, HALF)
        remote(
            gbuf.at[f, i, part], gbuf.at[f, i, part], ssend2.at[0], srecv2.at[(f * 8 + i) * 2 + h], dev(flip=True)
        ).wait_recv()

    def own_out(f, h):
        for n, dy in enumerate((1, 3) if h == 0 else (3, 1)):
            ring(f, 0, h, (4 - dy) % 4 * 2, dev(0, dy), h * 3 + n)
        ring(f, 0, h, 1, dev(flip=True), h * 3 + 2)

    def take(f, dy, h):
        arrive(f, dy * 2, h)
        if (dy, h) == (3, 0):
            ring(f, dy * 2, h, 4, dev(0, 1), 6)
        if (dy, h) == (1, 1):
            ring(f, dy * 2, h, 4, dev(0, 3), 7)
        ring(f, dy * 2, h, dy * 2 + 1, dev(flip=True), 8 + (dy - 1) * 2 + h)

    for h in range(2):
        part = pl.ds(h * HALF, HALF)
        mean = (acc[part, :] * inverse).astype(BF16)
        bbuf[part, :] = mean
        pre = base[part, :] + dot(mean, wmv[...])
        sig = jax.nn.sigmoid(pre)
        grad = (cotv[part, :].astype(F32) * sig * (1.0 + pre * (1.0 - sig))).astype(BF16)
        for f in range(PIECES):
            gbuf[f, 0, part, :] = grad[:, f * WIDE:(f + 1) * WIDE]
        own_out(0, h)
        updv[part, :] = (tv[part, :].astype(F32) + pre * sig).astype(BF16)
    out_u = pltpu.make_async_copy(updv, upd_hbm, lsem.at[5])
    out_u.start()

    grads = jnp.concatenate([gbuf[f, 0] for f in range(PIECES)], axis=1)
    is_self = c == 0
    t_val, b_val = tv[...], bbuf[...]
    give[...] = dot(jnp.where(is_self, b_val, t_val), grads, 0, 0).astype(BF16)
    to_sib = remote(give, got, gsem.at[0], gsem.at[1], dev(flip=True))
    to_sib.start()
    sends.append(to_sib)
    base[...] = dot(jnp.where(is_self, t_val, b_val), grads, 0, 0)

    to_sib.wait_recv()
    wsend[...] = (base[...] + got[...].astype(F32)).astype(BF16).reshape(16, 32, 512)
    place = x * 4 + y
    for dx in range(1, XN):
        to_x = lax.rem(x + dx, XN)
        cp = remote(
            wsend.at[pl.ds(to_x * 4, 4)], wrecv.at[pl.ds(dx * 4 - 4, 4)], wssem.at[dx - 1], wrsem.at[dx - 1], dev(dx)
        )
        cp.start()
        sends.append(cp)

    tgv[...] = (cotv[...].astype(F32) + dot(grads, wsv[...], 1, 1)).astype(BF16)
    out_t = pltpu.make_async_copy(tgv, tg_hbm, lsem.at[6])
    out_t.start()

    def scatter(f, dy, core):
        i = dy * 2 + core
        added = dot(links[i], gbuf[f, i]) * scale[i:i + 1, :1]
        terms[f] = added if i == 0 else terms[f] + added

    def gather_piece(f):
        scatter(f, 0, 0)
        for h in range(2):
            arrive(f, 1, h)
        scatter(f, 0, 1)
        take(f, 3, 0)
        take(f, 1, 1)
        take(f, 3, 1)
        take(f, 1, 0)
        if f + 1 < PIECES:
            own_out(f + 1, 0)
            own_out(f + 1, 1)
        scatter(f, 3, 0)
        scatter(f, 1, 0)
        if f == 0:
            weights_y()
        for i in (7, 3):
            for h in range(2):
                arrive(f, i, h)
            scatter(f, i // 2, 1)
        take(f, 2, 0)
        take(f, 2, 1)
        scatter(f, 2, 0)
        for h in range(2):
            arrive(f, 5, h)
        scatter(f, 2, 1)

    def x_out(f):
        xsend[f] = terms[f].astype(BF16).reshape(2, 2, HALF, WIDE)
        for dx in range(1, XN):
            xh = lax.div(lax.rem(x + dx, XN), 2)
            cp = remote(
                xsend.at[f, dx % 2, xh], xrecv.at[f, dx - 1], xssem.at[f * 3 + dx - 1], xrsem.at[f * 3 + dx - 1], dev(dx)
            )
            cp.start()
            sends.append(cp)

    def z_out(f):
        total = xsend[f, 0, lax.div(x, 2)].astype(F32)
        for i in range(XN - 1):
            remote(
                xrecv.at[f, i], xrecv.at[f, i], xssem.at[0], xrsem.at[f * 3 + i], dev(flip=True)
            ).wait_recv()
            total = total + xrecv[f, i].astype(F32)
        dsend[f] = total.astype(BF16).reshape(8, 32, WIDE)
        for dz in range(1, ZN):
            n = f * 7 + dz - 1
            cp = remote(
                dsend.at[f, lax.rem(z + dz, ZN)], drecv.at[f, dz - 1], dssem.at[n], drsem.at[n], dev(dz=dz)
            )
            cp.start()
            sends.append(cp)

    def finish(f):
        total = dsend[f, z].astype(F32)
        for i in range(ZN - 1):
            remote(
                drecv.at[f, i], drecv.at[f, i], dssem.at[0], drsem.at[f * 7 + i], dev(flip=True)
            ).wait_recv()
            total = total + drecv[f, i].astype(F32)
        return dot(total.astype(BF16), wmv[:, f * WIDE:(f + 1) * WIDE], 1, 1)

    def weights_y():
        total = wsend[pl.ds(x * 4, 4)].astype(F32)
        for i in range(XN - 1):
            got_x = wrecv.at[pl.ds(i * 4, 4)]
            remote(got_x, got_x, wssem.at[0], wrsem.at[i], dev(flip=True)).wait_recv()
            total = total + got_x[...].astype(F32)
        ysend[...] = total.astype(BF16)
        for dy in range(1, YN):
            cp = remote(
                ysend.at[lax.rem(y + dy, YN)], yrecv.at[dy - 1], wssem.at[2 + dy], wrsem.at[2 + dy], dev(0, dy)
            )
            cp.start()
            sends.append(cp)

    def weights_z():
        total = ysend[y].astype(F32)
        for i in range(YN - 1):
            remote(yrecv.at[i], yrecv.at[i], wssem.at[0], wrsem.at[3 + i], dev(flip=True)).wait_recv()
            total = total + yrecv[i].astype(F32)
        zbuf[z] = total.astype(BF16)
        for dz in range(1, ZN):
            cp = remote(zbuf.at[z], zbuf.at[z], zssem.at[dz], zrsem.at[z], dev(0, 0, dz))
            cp.start()
            sends.append(cp)

    def weights_out():
        for dz in range(1, ZN):
            peer = lax.rem(z + dz, ZN)
            remote(zbuf.at[peer], zbuf.at[peer], zssem.at[dz], zrsem.at[peer], dev(flip=True)).wait_recv()
        total = zbuf[0].astype(F32)
        for i in range(1, ZN):
            total = total + zbuf[i].astype(F32)
        wres[c, place] = total.astype(BF16)
        for i, (dx, dy) in enumerate(plane):
            cp = remote(wres.at[c, place], wres.at[c, place], assem.at[i], arsem.at[i], dev(dx, dy))
            cp.start()
            sends.append(cp)

    gather_piece(0)
    x_out(0)
    weights_z()
    for f in range(1, PIECES):
        gather_piece(f)
        x_out(f)
        z_out(f - 1)
        if f == 1:
            weights_out()
    out = finish(0)
    for f in range(1, PIECES - 1):
        out = out + finish(f)
    z_out(PIECES - 1)

    for i, (dx, dy) in enumerate(plane):
        peer = lax.rem(x + (XN - dx), XN) * 4 + lax.rem(y + (YN - dy), YN)
        remote(wres.at[c, peer], wres.at[c, peer], assem.at[i], arsem.at[i], dev(flip=True)).wait_recv()
    cross = remote(wres.at[c], wres.at[c], bssem, brsem, dev(flip=True))
    cross.start()
    sends.append(cross)

    sg_ref[...] = (out + finish(PIECES - 1)).astype(BF16)

    remote(wres.at[1 - c], wres.at[1 - c], bssem, brsem, dev(flip=True)).wait_recv()
    out_w = pltpu.make_async_copy(wres, w_out, lsem.at[7])
    out_w.start()
    for cp in sends:
        cp.wait_send()
    out_u.wait()
    out_t.wait()
    out_w.wait()


def place_outputs(upd, tg, sg, w, upd_out, tg_out, sg_out, self_out, message_out):
    upd_out[...] = upd[...]
    tg_out[...] = tg[...]
    sg_out[...] = sg[...]
    rows = w.shape[1] * 32
    self_out[...] = w[0].reshape(rows, 512).astype(F32) * 131072 ** (-0.5)
    message_out[...] = w[1].reshape(rows, 512).astype(F32) * 8192 ** (-0.5)


def local(
    source_table, target_table, message_weight, self_weight, tile_lists, key_offsets, list_lengths, cotangent
):
    any_spec = pl.BlockSpec(memory_space=pl.ANY)
    vmem = pl.BlockSpec(memory_space=pltpu.VMEM)
    dma = pltpu.SemaphoreType.DMA
    square = (512, 512)
    updated, target_gradient, source_gradient, weights = pl.pallas_call(
        kernel,
        out_shape=(
            jax.ShapeDtypeStruct(square, BF16),
            jax.ShapeDtypeStruct(square, BF16),
            jax.ShapeDtypeStruct((32, 512), BF16),
            jax.ShapeDtypeStruct((2, 16, 32, 512), BF16),
        ),
        in_specs=[any_spec, any_spec, any_spec, any_spec, vmem, vmem, vmem, any_spec],
        out_specs=(any_spec, any_spec, vmem, any_spec),
        scratch_shapes=[
            pltpu.VMEM((16, 4, 128, 512), BF16),
            pltpu.VMEM((PIECES, 8, 512, WIDE), BF16),
            pltpu.VMEM((8, 32, 512), BF16),
            pltpu.VMEM((8, 1024, 512), BF16),
            pltpu.VMEM((8, 128), F32),
            pltpu.VMEM(square, BF16),
            pltpu.VMEM(square, BF16),
            pltpu.VMEM(square, BF16),
            pltpu.VMEM(square, BF16),
            pltpu.VMEM(square, F32),
            pltpu.VMEM(square, F32),
            pltpu.VMEM(square, BF16),
            pltpu.VMEM(square, BF16),
            pltpu.VMEM(square, BF16),
            pltpu.VMEM((512, 16), F32),
            pltpu.VMEM((PIECES, 1024, WIDE), F32),
            pltpu.VMEM(square, BF16),
            pltpu.VMEM(square, BF16),
            pltpu.VMEM((16, 32, 512), BF16),
            pltpu.VMEM((12, 32, 512), BF16),
            pltpu.VMEM((4, 32, 512), BF16),
            pltpu.VMEM((3, 32, 512), BF16),
            pltpu.VMEM((8, 32, 512), BF16),
            pltpu.VMEM((2, 16, 32, 512), BF16),
            pltpu.VMEM((PIECES, 2, 2, HALF, WIDE), BF16),
            pltpu.VMEM((PIECES, 3, HALF, WIDE), BF16),
            pltpu.VMEM((PIECES, 8, 32, WIDE), BF16),
            pltpu.VMEM((PIECES, 7, 32, WIDE), BF16),
            dma((8,)),
            dma((60,)), dma((64,)),
            dma((7,)), dma((8,)),
            dma((14 * PIECES,)), dma((16 * PIECES,)),
            dma((2,)),
            dma((6,)), dma((6,)),
            dma((8,)), dma((8,)),
            dma((15,)), dma((15,)),
            dma(()), dma(()),
            dma((3 * PIECES,)), dma((3 * PIECES,)),
            dma((7 * PIECES,)), dma((7 * PIECES,)),
        ],
        compiler_params=pltpu.CompilerParams(
            collective_id=0, has_side_effects=True, vmem_limit_bytes=56 * 1024 * 1024
        ),
    )(
        source_table.reshape(4, 128, 512), target_table, message_weight, self_weight, tile_lists, key_offsets.T,
        list_lengths.reshape(1, 1), cotangent,
    )
    steps = 4
    rows = 512 // steps
    wide = pl.BlockSpec((rows, 512), lambda i: (i, 0))
    small = pl.BlockSpec((32, 512), lambda i: (0, 0))
    return pl.pallas_call(
        place_outputs,
        grid=(steps,),
        out_shape=(
            jax.ShapeDtypeStruct(square, BF16),
            jax.ShapeDtypeStruct(square, BF16),
            jax.ShapeDtypeStruct((32, 512), BF16),
            jax.ShapeDtypeStruct(square, F32),
            jax.ShapeDtypeStruct(square, F32),
        ),
        in_specs=[wide, wide, small, pl.BlockSpec((2, rows // 32, 32, 512), lambda i: (0, i, 0, 0))],
        out_specs=(wide, wide, small, wide, wide),
    )(updated, target_gradient, source_gradient, weights)


def solution(mesh):
    placed = (
        P("blk", None),
        P(("row", "blk"), None),
        P(),
        P(),
        P(("row", "blk"), None),
        P(("row", "blk"), None),
        P(("row", "blk")),
        P(("row", "blk"), None),
    )
    return jax.shard_map(
        local,
        mesh=mesh,
        in_specs=placed,
        out_specs=(
            P(("row", "blk"), None),
            P(("row", "blk"), None),
            P(("blk", "row"), None),
            P(),
            P(),
        ),
        check_vma=False,
    )
```

```python
import functools

import jax
import jax.numpy as jnp
from jax import lax
from jax.experimental import pallas as pl
from jax.experimental.pallas import tpu as pltpu
from jax.sharding import PartitionSpec as P

XN, YN, ZN = 4, 4, 8
HALF = 256
PIECES = 2
WIDE = 512 // PIECES
F32 = jnp.float32
BF16 = jnp.bfloat16


def dot(a, b, ca=1, cb=0):
    return lax.dot_general(a, b, (((ca,), (cb,)), ((), ())), preferred_element_type=F32)


def slot(col, dy, core):
    return col * 8 + dy * 2 + core


def kernel(
    s_hbm, t_hbm, wm_hbm, ws_hbm, lists_ref, ko_ref, len_ref, cot_hbm,
    updv, tgv, sg_ref, self_ref, message_ref,
    sbuf, gbuf, nsend, notes, links, scale, tv, cotv, wmv, wsv, acc, base, bbuf, koff, terms,
    give, got, wsend, wrecv, ysend, yrecv, zbuf, wres, xsend, xrecv, dsend, drecv,
    lsem, ssend1, srecv1, nssem, nrsem, ssend2, srecv2, gsem, wssem, wrsem, zssem, zrsem, assem, arsem, bssem, brsem,
    xssem, xrsem, dssem, drsem, near_sem, far_sem,
):
    r = lax.axis_index("row")
    b = lax.axis_index("blk")
    x = lax.div(r, 8) * 2 + lax.div(b, 8)
    y = lax.rem(lax.div(b, 2), 4)
    z = lax.rem(r, 8)
    c = lax.rem(b, 2)

    def dev(dx=0, dy=0, dz=0, flip=False):
        xx = lax.rem(x + dx, XN)
        yy = lax.rem(y + dy, YN)
        zz = lax.rem(z + dz, ZN)
        cc = 1 - c if flip else c
        return {"row": lax.div(xx, 2) * 8 + zz, "blk": lax.rem(xx, 2) * 8 + yy * 2 + cc}

    def remote(src, dst, ss, rs, to):
        return pltpu.make_async_remote_copy(
            src_ref=src, dst_ref=dst, send_sem=ss, recv_sem=rs,
            device_id=to, device_id_type=pl.DeviceIdType.MESH,
        )

    loads = {}
    for i, (name, src, dst) in enumerate((
        ("s", s_hbm, sbuf.at[0]), ("t", t_hbm, tv), ("ws", ws_hbm, wsv), ("wm", wm_hbm, wmv), ("cot", cot_hbm, cotv),
    )):
        loads[name] = pltpu.make_async_copy(src, dst, lsem.at[i])
        loads[name].start()

    plane = [(dx, dy) for dx in range(XN) for dy in range(YN) if (dx, dy) != (0, 0)]
    nearest = [dev(flip=True), dev(1), dev(3), dev(0, 1), dev(0, 3), dev(dz=1), dev(dz=ZN - 1)]

    def meet(sem, others):
        for to in others:
            pl.semaphore_signal(sem, inc=1, device_id=to, device_id_type=pl.DeviceIdType.MESH)
        pl.semaphore_wait(sem, len(others))

    meet(pltpu.get_barrier_semaphore(), nearest)

    sends = []

    def settle():
        for cp in sends:
            cp.wait_send()
        sends.clear()


    parity = lax.rem(z, 2)
    made = [0]

    def part_of(t, role):
        base_row = 2 * parity if role < 2 else 2 - 2 * parity
        return sbuf.at[t, base_row + role % 2]

    def push(t, role, to_t, to_role, to):
        cp = remote(part_of(t, role), part_of(to_t, role), ssend1.at[made[0]], srecv1.at[to_t * 4 + to_role], to)
        cp.start()
        made[0] += 1
        sends.append(cp)

    def got_part(col, dy, core, role):
        t = slot(col, dy, core)
        remote(part_of(t, role), part_of(t, role), ssend1.at[0], srecv1.at[t * 4 + role], dev(flip=True)).wait_recv()

    def half_of(t, pair):
        return sbuf.at[t, pl.ds(2 * parity if pair == 0 else 2 - 2 * parity, 2)]

    def push_half(t, to_t, pair):
        half = half_of(t, pair)
        cp = remote(half, half_of(to_t, pair), ssend1.at[made[0]], srecv1.at[to_t * 4 + 2 * pair], dev(flip=True))
        cp.start()
        made[0] += 1
        sends.append(cp)

    def got_tile(col, dy):
        t = slot(col, dy, 1)
        for pair in range(2):
            half = half_of(t, pair)
            remote(half, half, ssend1.at[0], srecv1.at[t * 4 + 2 * pair], dev(flip=True)).wait_recv()

    here = set()

    def fetch(col, dy, role):
        got_part(col, dy, 0, role)
        t = slot(col, dy, 0)
        if col == 0 and dy == 3 and role in (0, 2):
            push(t, role, slot(0, 2, 0), role, dev(0, 1))
        if col == 0 and dy == 1 and role in (1, 3):
            push(t, role, slot(0, 2, 0), role, dev(0, 3))
        if role < 2 and (col, dy) not in ((0, 2), (1, 0)):
            push(t, role, t, role + 2, dev(dz=ZN - 1 if role == 0 else 1))
        if role < 2 and col == 0:
            push(t, role, slot(1, dy, 0), role, dev(1 if role == 0 else 3))
        here.add((t, role))
        if (t, role ^ 1) in here:
            push_half(t, slot(col, dy, 1), role // 2)

    loads["s"].wait()
    for role in (0, 1):
        push(0, role, slot(0, 3, 0), role, dev(0, 1))
        push(0, 1 - role, slot(0, 1, 0), 1 - role, dev(0, 3))
        push(0, 2 * role, slot(1, 0, 0), 2 * role, dev(1))
        push(0, 2 * role + 1, slot(1, 0, 0), 2 * role + 1, dev(3))
    for pair in range(2):
        push_half(0, slot(0, 0, 1), pair)

    k_row = lax.broadcasted_iota(jnp.int32, (16, 16), 0)
    s_col = lax.broadcasted_iota(jnp.int32, (16, 16), 1)
    kc, kd, ke = k_row // 8, (k_row // 2) % 4, k_row % 2
    xl = lax.rem(x, 2)
    tile_id = ((xl + kc) % 2) * 8 + ((y + kd) % 4) * 2 + (c + ke) % 2
    pick = ((lists_ref[...] == tile_id) & (s_col < len_ref[...])).astype(F32).astype(BF16)
    keys = ko_ref[...] + 1
    k_hi = (keys // 256).astype(F32).astype(BF16)
    k_lo = (keys % 256).astype(F32).astype(BF16)
    koff[...] = dot(k_hi, pick, 0, 1) * 256.0 + dot(k_lo, pick, 0, 1) - 1.0
    length = len_ref[...].astype(F32)
    inverse = 1.0 / length
    meet(near_sem, nearest)
    meet(far_sem, [dev(2), dev(0, 2), dev(dz=2), dev(dz=ZN - 2)])
    keys_t = dot(pick, k_hi) * 256.0 + dot(pick, k_lo) - 1.0
    for i in range(8):
        nsend[i, 0:1, :] = keys_t[i:i + 1, :]
        nsend[i, 1:2, :] = keys_t[8 + i:9 + i, :]
        nsend[i, 2:3, :] = jnp.broadcast_to(inverse, (1, 512))
    for i in range(1, 8):
        dy, core = i // 2, i % 2
        to = slot(0, (4 - dy) % 4, core)
        cp = remote(nsend.at[i], notes.at[to], nssem.at[i - 1], nrsem.at[to], dev(0, dy, flip=core == 1))
        cp.start()
        sends.append(cp)

    loads["t"].wait()
    loads["ws"].wait()
    base[...] = dot(tv[...], wsv[...])

    lanes = lax.broadcasted_iota(jnp.int32, (512, 512), 1).astype(F32)

    def gather_tile(t, init=False):
        pattern = jnp.where(koff[:, t:t + 1] == lanes, 1.0, 0.0).astype(BF16)
        added = dot(pattern, sbuf[t].reshape(512, 512))
        acc[...] = added if init else acc[...] + added

    sub = lax.broadcasted_iota(jnp.int32, (512, 512), 0).astype(F32)

    def link_tile(i):
        if i:
            remote(notes.at[i], notes.at[i], nssem.at[0], nrsem.at[i], dev(flip=True)).wait_recv()
        note = nsend if i == 0 else notes
        for col in range(2):
            links[i, col * 512:(col + 1) * 512, :] = jnp.where(note[i, col:col + 1, :] == sub, 1.0, 0.0).astype(BF16)
        scale[i:i + 1, :] = note[i, 2:3, :128]

    gather_tile(slot(0, 0, 0), True)
    link_tile(0)
    fetch(0, 3, 0)
    fetch(0, 1, 1)
    fetch(1, 0, 0)
    fetch(1, 0, 1)
    got_tile(0, 0)
    gather_tile(slot(0, 0, 1))
    fetch(0, 3, 1)
    fetch(0, 1, 0)
    fetch(1, 0, 2)
    fetch(1, 0, 3)
    gather_tile(slot(1, 0, 0))
    fetch(0, 3, 2)
    fetch(0, 1, 3)
    fetch(0, 2, 0)
    fetch(0, 2, 1)
    fetch(1, 3, 0)
    fetch(1, 1, 1)
    link_tile(1)
    link_tile(2)
    fetch(0, 1, 2)
    fetch(0, 3, 3)
    gather_tile(slot(0, 1, 0))
    fetch(1, 1, 0)
    fetch(1, 3, 1)
    gather_tile(slot(0, 3, 0))
    fetch(0, 2, 2)
    fetch(0, 2, 3)
    fetch(1, 3, 2)
    fetch(1, 1, 3)
    gather_tile(slot(0, 2, 0))
    fetch(1, 2, 0)
    fetch(1, 2, 1)
    got_tile(1, 0)
    gather_tile(slot(1, 0, 1))
    fetch(1, 1, 2)
    fetch(1, 3, 3)
    for dy in (1, 3, 2):
        got_tile(0, dy)
        gather_tile(slot(0, dy, 1))
    gather_tile(slot(1, 1, 0))
    gather_tile(slot(1, 3, 0))
    for i in range(3, 8):
        link_tile(i)
    fetch(1, 2, 2)
    fetch(1, 2, 3)
    for dy in (1, 3):
        got_tile(1, dy)
        gather_tile(slot(1, dy, 1))
    gather_tile(slot(1, 2, 0))
    got_tile(1, 2)
    gather_tile(slot(1, 2, 1))

    loads["wm"].wait()
    loads["cot"].wait()

    def ring(f, i, h, to_i, to, n):
        part = pl.ds(h * HALF, HALF)
        k = (f * 8 + to_i) * 2 + h
        cp = remote(gbuf.at[f, i, part], gbuf.at[f, to_i, part], ssend2.at[f * 14 + n], srecv2.at[k], to)
        cp.start()
        sends.append(cp)

    def arrive(f, i, h):
        part = pl.ds(h * HALF, HALF)
        remote(
            gbuf.at[f, i, part], gbuf.at[f, i, part], ssend2.at[0], srecv2.at[(f * 8 + i) * 2 + h], dev(flip=True)
        ).wait_recv()

    def own_out(f, h):
        outs = ((1, 0),) if h == 0 else ((3, 1), (3, 0), (1, 1))
        for dy, half in outs:
            ring(f, 0, half, (4 - dy) % 4 * 2, dev(0, dy), half * 2 + dy // 2)
        ring(f, 0, h, 1, dev(flip=True), 4 + h)

    def take(f, dy, h):
        arrive(f, dy * 2, h)
        if (dy, h) == (3, 0):
            ring(f, dy * 2, h, 4, dev(0, 1), 6)
        if (dy, h) == (1, 1):
            ring(f, dy * 2, h, 4, dev(0, 3), 7)
        ring(f, dy * 2, h, dy * 2 + 1, dev(flip=True), 8 + (dy - 1) * 2 + h)

    for h in range(2):
        part = pl.ds(h * HALF, HALF)
        mean = (acc[part, :] * inverse).astype(BF16)
        bbuf[part, :] = mean
        pre = base[part, :] + dot(mean, wmv[...])
        sig = jax.nn.sigmoid(pre)
        grad = (cotv[part, :].astype(F32) * sig * (1.0 + pre * (1.0 - sig))).astype(BF16)
        for f in range(PIECES):
            gbuf[f, 0, part, :] = grad[:, f * WIDE:(f + 1) * WIDE]
        own_out(0, h)
        updv[part, :] = (tv[part, :].astype(F32) + pre * sig).astype(BF16)

    grads = jnp.concatenate([gbuf[f, 0] for f in range(PIECES)], axis=1)
    is_self = c == 0
    t_val, b_val = tv[...], bbuf[...]
    give[...] = dot(jnp.where(is_self, b_val, t_val), grads, 0, 0).astype(BF16)
    to_sib = remote(give, got, gsem.at[0], gsem.at[1], dev(flip=True))
    to_sib.start()
    sends.append(to_sib)
    base[...] = dot(jnp.where(is_self, t_val, b_val), grads, 0, 0)

    to_sib.wait_recv()
    wsend[...] = (base[...] + got[...].astype(F32)).astype(BF16).reshape(16, 32, 512)
    place = x * 4 + y
    for dx in range(1, XN):
        to_x = lax.rem(x + dx, XN)
        cp = remote(
            wsend.at[pl.ds(to_x * 4, 4)], wrecv.at[pl.ds(dx * 4 - 4, 4)], wssem.at[dx - 1], wrsem.at[dx - 1], dev(dx)
        )
        cp.start()
        sends.append(cp)

    tgv[...] = (cotv[...].astype(F32) + dot(grads, wsv[...], 1, 1)).astype(BF16)

    def scatter(f, dy, core):
        i = dy * 2 + core
        added = dot(links[i], gbuf[f, i]) * scale[i:i + 1, :1]
        terms[f] = added if i == 0 else terms[f] + added

    def gather_piece(f):
        scatter(f, 0, 0)
        for h in range(2):
            arrive(f, 1, h)
        scatter(f, 0, 1)
        take(f, 3, 0)
        take(f, 1, 1)
        take(f, 3, 1)
        take(f, 1, 0)
        if f + 1 < PIECES:
            own_out(f + 1, 0)
            own_out(f + 1, 1)
        scatter(f, 3, 0)
        scatter(f, 1, 0)
        if f == 0:
            for cp in old:
                cp.wait_send()
            weights_y()
        for i in (7, 3):
            for h in range(2):
                arrive(f, i, h)
            scatter(f, i // 2, 1)
        take(f, 2, 0)
        take(f, 2, 1)
        scatter(f, 2, 0)
        for h in range(2):
            arrive(f, 5, h)
        scatter(f, 2, 1)

    def x_out(f):
        xsend[f] = terms[f].astype(BF16).reshape(2, 2, HALF, WIDE)
        for dx in range(1, XN):
            xh = lax.div(lax.rem(x + dx, XN), 2)
            cp = remote(
                xsend.at[f, dx % 2, xh], xrecv.at[f, dx - 1], xssem.at[f * 3 + dx - 1], xrsem.at[f * 3 + dx - 1], dev(dx)
            )
            cp.start()
            sends.append(cp)

    def z_out(f):
        total = xsend[f, 0, lax.div(x, 2)].astype(F32)
        for i in range(XN - 1):
            remote(
                xrecv.at[f, i], xrecv.at[f, i], xssem.at[0], xrsem.at[f * 3 + i], dev(flip=True)
            ).wait_recv()
            total = total + xrecv[f, i].astype(F32)
        dsend[f] = total.astype(BF16).reshape(8, 32, WIDE)
        for dz in range(1, ZN):
            n = f * 7 + dz - 1
            cp = remote(
                dsend.at[f, lax.rem(z + dz, ZN)], drecv.at[f, dz - 1], dssem.at[n], drsem.at[n], dev(dz=dz)
            )
            cp.start()
            sends.append(cp)

    def finish(f):
        total = dsend[f, z].astype(F32)
        for i in range(ZN - 1):
            remote(
                drecv.at[f, i], drecv.at[f, i], dssem.at[0], drsem.at[f * 7 + i], dev(flip=True)
            ).wait_recv()
            total = total + drecv[f, i].astype(F32)
        return dot(total.astype(BF16), wmv[:, f * WIDE:(f + 1) * WIDE], 1, 1)

    def weights_y():
        total = wsend[pl.ds(x * 4, 4)].astype(F32)
        for i in range(XN - 1):
            got_x = wrecv.at[pl.ds(i * 4, 4)]
            remote(got_x, got_x, wssem.at[0], wrsem.at[i], dev(flip=True)).wait_recv()
            total = total + got_x[...].astype(F32)
        ysend[...] = total.astype(BF16)
        for dy in range(1, YN):
            cp = remote(
                ysend.at[lax.rem(y + dy, YN)], yrecv.at[dy - 1], wssem.at[2 + dy], wrsem.at[2 + dy], dev(0, dy)
            )
            cp.start()
            sends.append(cp)

    def weights_z():
        total = ysend[y].astype(F32)
        for i in range(YN - 1):
            remote(yrecv.at[i], yrecv.at[i], wssem.at[0], wrsem.at[3 + i], dev(flip=True)).wait_recv()
            total = total + yrecv[i].astype(F32)
        zbuf[z] = total.astype(BF16)
        for dz in range(1, ZN):
            cp = remote(zbuf.at[z], zbuf.at[z], zssem.at[dz], zrsem.at[z], dev(0, 0, dz))
            cp.start()
            sends.append(cp)

    def weights_out():
        for dz in range(1, ZN):
            peer = lax.rem(z + dz, ZN)
            remote(zbuf.at[peer], zbuf.at[peer], zssem.at[dz], zrsem.at[peer], dev(flip=True)).wait_recv()
        total = zbuf[0].astype(F32)
        for i in range(1, ZN):
            total = total + zbuf[i].astype(F32)
        wres[c, place] = total.astype(BF16)
        for i, (dx, dy) in enumerate(plane):
            cp = remote(wres.at[c, place], wres.at[c, place], assem.at[i], arsem.at[i], dev(dx, dy))
            cp.start()
            sends.append(cp)

    old = list(sends)
    sends.clear()
    gather_piece(0)
    x_out(0)
    weights_z()
    for f in range(1, PIECES):
        gather_piece(f)
        x_out(f)
        z_out(f - 1)
        if f == 1:
            settle()
            weights_out()
    out = finish(0)
    for f in range(1, PIECES - 1):
        out = out + finish(f)
    z_out(PIECES - 1)

    for i, (dx, dy) in enumerate(plane):
        peer = lax.rem(x + (XN - dx), XN) * 4 + lax.rem(y + (YN - dy), YN)
        remote(wres.at[c, peer], wres.at[c, peer], assem.at[i], arsem.at[i], dev(flip=True)).wait_recv()
    cross = remote(wres.at[c], wres.at[c], bssem, brsem, dev(flip=True))
    cross.start()
    sends.append(cross)

    sg_ref[...] = (out + finish(PIECES - 1)).astype(BF16)

    def self_done():
        self_ref[...] = wres[0].reshape(512, 512).astype(F32) * 131072 ** (-0.5)

    def message_done():
        message_ref[...] = wres[1].reshape(512, 512).astype(F32) * 8192 ** (-0.5)

    pl.when(c == 0)(self_done)
    pl.when(c == 1)(message_done)
    remote(wres.at[1 - c], wres.at[1 - c], bssem, brsem, dev(flip=True)).wait_recv()
    pl.when(c == 1)(self_done)
    pl.when(c == 0)(message_done)
    settle()


def place_outputs(*refs):
    count = len(refs) // 2
    copies = [pltpu.make_async_copy(refs[i], refs[count + i], refs[-1].at[i]) for i in range(count)]
    for cp in copies:
        cp.start()
    for cp in copies:
        cp.wait()


def local(
    source_table, target_table, message_weight, self_weight, tile_lists, key_offsets, list_lengths, cotangent
):
    any_spec = pl.BlockSpec(memory_space=pl.ANY)
    vmem = pl.BlockSpec(memory_space=pltpu.VMEM)
    dma = pltpu.SemaphoreType.DMA
    square = (512, 512)
    shapes = ((square, BF16), (square, BF16), ((32, 512), BF16), (square, F32), (square, F32))
    held = pl.pallas_call(
        kernel,
        out_shape=tuple(pltpu.VMEM(*shape) for shape in shapes),
        in_specs=[any_spec, any_spec, any_spec, any_spec, vmem, vmem, vmem, any_spec],
        out_specs=(vmem,) * 5,
        scratch_shapes=[
            pltpu.VMEM((16, 4, 128, 512), BF16),
            pltpu.VMEM((PIECES, 8, 512, WIDE), BF16),
            pltpu.VMEM((8, 8, 512), F32),
            pltpu.VMEM((8, 8, 512), F32),
            pltpu.VMEM((8, 1024, 512), BF16),
            pltpu.VMEM((8, 128), F32),
            pltpu.VMEM(square, BF16),
            pltpu.VMEM(square, BF16),
            pltpu.VMEM(square, BF16),
            pltpu.VMEM(square, BF16),
            pltpu.VMEM(square, F32),
            pltpu.VMEM(square, F32),
            pltpu.VMEM(square, BF16),
            pltpu.VMEM((512, 16), F32),
            pltpu.VMEM((PIECES, 1024, WIDE), F32),
            pltpu.VMEM(square, BF16),
            pltpu.VMEM(square, BF16),
            pltpu.VMEM((16, 32, 512), BF16),
            pltpu.VMEM((12, 32, 512), BF16),
            pltpu.VMEM((4, 32, 512), BF16),
            pltpu.VMEM((3, 32, 512), BF16),
            pltpu.VMEM((8, 32, 512), BF16),
            pltpu.VMEM((2, 16, 32, 512), BF16),
            pltpu.VMEM((PIECES, 2, 2, HALF, WIDE), BF16),
            pltpu.VMEM((PIECES, 3, HALF, WIDE), BF16),
            pltpu.VMEM((PIECES, 8, 32, WIDE), BF16),
            pltpu.VMEM((PIECES, 7, 32, WIDE), BF16),
            dma((5,)),
            dma((44,)), dma((64,)),
            dma((7,)), dma((8,)),
            dma((14 * PIECES,)), dma((16 * PIECES,)),
            dma((2,)),
            dma((6,)), dma((6,)),
            dma((8,)), dma((8,)),
            dma((15,)), dma((15,)),
            dma(()), dma(()),
            dma((3 * PIECES,)), dma((3 * PIECES,)),
            dma((7 * PIECES,)), dma((7 * PIECES,)),
            pltpu.SemaphoreType.REGULAR, pltpu.SemaphoreType.REGULAR,
        ],
        compiler_params=pltpu.CompilerParams(
            collective_id=0, has_side_effects=True, vmem_limit_bytes=56 * 1024 * 1024
        ),
    )(
        source_table.reshape(4, 128, 512), target_table, message_weight, self_weight, tile_lists, key_offsets.T,
        list_lengths.reshape(1, 1), cotangent,
    )
    return pl.pallas_call(
        place_outputs,
        out_shape=tuple(jax.ShapeDtypeStruct(*shape) for shape in shapes),
        in_specs=[vmem] * 5,
        out_specs=(any_spec,) * 5,
        scratch_shapes=[dma((5,))],
    )(*[pltpu.with_memory_space_constraint(one, pltpu.VMEM) for one in held])


def solution(mesh):
    placed = (
        P("blk", None),
        P(("row", "blk"), None),
        P(),
        P(),
        P(("row", "blk"), None),
        P(("row", "blk"), None),
        P(("row", "blk")),
        P(("row", "blk"), None),
    )
    return jax.shard_map(
        local,
        mesh=mesh,
        in_specs=placed,
        out_specs=(
            P(("row", "blk"), None),
            P(("row", "blk"), None),
            P(("blk", "row"), None),
            P(),
            P(),
        ),
        check_vma=False,
    )
```

```python
import functools

import jax
import jax.numpy as jnp
from jax import lax
from jax.experimental import pallas as pl
from jax.experimental.pallas import tpu as pltpu
from jax.sharding import PartitionSpec as P

XN, YN, ZN = 4, 4, 8
HALF = 256
PIECES = 2
WIDE = 512 // PIECES
F32 = jnp.float32
BF16 = jnp.bfloat16


def dot(a, b, ca=1, cb=0):
    return lax.dot_general(a, b, (((ca,), (cb,)), ((), ())), preferred_element_type=F32)


def slot(col, dy, core):
    return col * 8 + dy * 2 + core


def kernel(
    s_hbm, t_hbm, wm_hbm, ws_hbm, lists_ref, ko_ref, len_ref, cot_hbm,
    updv, tgv, sg_ref, self_ref, message_ref,
    sbuf, gbuf, nsend, notes, links, scale, tv, cotv, wmv, wsv, acc, base, bbuf, koff, terms,
    give, got, wsend, wrecv, ysend, yrecv, zbuf, wres, xsend, xrecv, dsend, drecv,
    lsem, ssend1, srecv1, nssem, nrsem, ssend2, srecv2, gsem, wssem, wrsem, zssem, zrsem, assem, arsem, bssem, brsem,
    xssem, xrsem, dssem, drsem, near_sem, far_sem,
):
    r = lax.axis_index("row")
    b = lax.axis_index("blk")
    x = lax.div(r, 8) * 2 + lax.div(b, 8)
    y = lax.rem(lax.div(b, 2), 4)
    z = lax.rem(r, 8)
    c = lax.rem(b, 2)

    def dev(dx=0, dy=0, dz=0, flip=False):
        xx = lax.rem(x + dx, XN)
        yy = lax.rem(y + dy, YN)
        zz = lax.rem(z + dz, ZN)
        cc = 1 - c if flip else c
        return {"row": lax.div(xx, 2) * 8 + zz, "blk": lax.rem(xx, 2) * 8 + yy * 2 + cc}

    def remote(src, dst, ss, rs, to):
        return pltpu.make_async_remote_copy(
            src_ref=src, dst_ref=dst, send_sem=ss, recv_sem=rs,
            device_id=to, device_id_type=pl.DeviceIdType.MESH,
        )

    loads = {}
    for i, (name, src, dst) in enumerate((
        ("s", s_hbm, sbuf.at[0]), ("t", t_hbm, tv), ("ws", ws_hbm, wsv), ("wm", wm_hbm, wmv), ("cot", cot_hbm, cotv),
    )):
        loads[name] = pltpu.make_async_copy(src, dst, lsem.at[i])
        loads[name].start()

    plane = [(dx, dy) for dx in range(XN) for dy in range(YN) if (dx, dy) != (0, 0)]
    nearest = [dev(flip=True), dev(1), dev(3), dev(0, 1), dev(0, 3), dev(dz=1), dev(dz=ZN - 1)]

    def meet(sem, others):
        for to in others:
            pl.semaphore_signal(sem, inc=1, device_id=to, device_id_type=pl.DeviceIdType.MESH)
        pl.semaphore_wait(sem, len(others))

    meet(pltpu.get_barrier_semaphore(), nearest)

    sends = []

    def settle():
        for cp in sends:
            cp.wait_send()
        sends.clear()


    parity = lax.rem(z, 2)
    made = [0]

    def part_of(t, role):
        base_row = 2 * parity if role < 2 else 2 - 2 * parity
        return sbuf.at[t, base_row + role % 2]

    def push(t, role, to_t, to_role, to):
        cp = remote(part_of(t, role), part_of(to_t, role), ssend1.at[made[0]], srecv1.at[to_t * 4 + to_role], to)
        cp.start()
        made[0] += 1
        sends.append(cp)

    def got_part(col, dy, core, role):
        t = slot(col, dy, core)
        remote(part_of(t, role), part_of(t, role), ssend1.at[0], srecv1.at[t * 4 + role], dev(flip=True)).wait_recv()

    def half_of(t, pair):
        return sbuf.at[t, pl.ds(2 * parity if pair == 0 else 2 - 2 * parity, 2)]

    def push_half(t, to_t, pair):
        half = half_of(t, pair)
        cp = remote(half, half_of(to_t, pair), ssend1.at[made[0]], srecv1.at[to_t * 4 + 2 * pair], dev(flip=True))
        cp.start()
        made[0] += 1
        sends.append(cp)

    def got_tile(col, dy):
        t = slot(col, dy, 1)
        for pair in range(2):
            half = half_of(t, pair)
            remote(half, half, ssend1.at[0], srecv1.at[t * 4 + 2 * pair], dev(flip=True)).wait_recv()

    here = set()

    def fetch(col, dy, role):
        got_part(col, dy, 0, role)
        t = slot(col, dy, 0)
        if col == 0 and dy == 3 and role in (0, 2):
            push(t, role, slot(0, 2, 0), role, dev(0, 1))
        if col == 0 and dy == 1 and role in (1, 3):
            push(t, role, slot(0, 2, 0), role, dev(0, 3))
        if role < 2 and (col, dy) not in ((0, 2), (1, 0)):
            push(t, role, t, role + 2, dev(dz=ZN - 1 if role == 0 else 1))
        if role < 2 and col == 0:
            push(t, role, slot(1, dy, 0), role, dev(1 if role == 0 else 3))
        here.add((t, role))
        if (t, role ^ 1) in here:
            push_half(t, slot(col, dy, 1), role // 2)

    loads["s"].wait()
    for role in (0, 1):
        push(0, role, slot(0, 3, 0), role, dev(0, 1))
        push(0, 1 - role, slot(0, 1, 0), 1 - role, dev(0, 3))
        push(0, 2 * role, slot(1, 0, 0), 2 * role, dev(1))
        push(0, 2 * role + 1, slot(1, 0, 0), 2 * role + 1, dev(3))
    for pair in range(2):
        push_half(0, slot(0, 0, 1), pair)

    k_row = lax.broadcasted_iota(jnp.int32, (16, 16), 0)
    s_col = lax.broadcasted_iota(jnp.int32, (16, 16), 1)
    kc, kd, ke = k_row // 8, (k_row // 2) % 4, k_row % 2
    xl = lax.rem(x, 2)
    tile_id = ((xl + kc) % 2) * 8 + ((y + kd) % 4) * 2 + (c + ke) % 2
    pick = ((lists_ref[...] == tile_id) & (s_col < len_ref[...])).astype(F32).astype(BF16)
    keys = ko_ref[...] + 1
    k_hi = (keys // 256).astype(F32).astype(BF16)
    k_lo = (keys % 256).astype(F32).astype(BF16)
    koff[...] = dot(k_hi, pick, 0, 1) * 256.0 + dot(k_lo, pick, 0, 1) - 1.0
    length = len_ref[...].astype(F32)
    inverse = 1.0 / length
    meet(near_sem, nearest)
    meet(far_sem, [dev(2), dev(0, 2), dev(dz=2), dev(dz=ZN - 2)])
    keys_t = dot(pick, k_hi) * 256.0 + dot(pick, k_lo) - 1.0
    for i in range(8):
        nsend[i, 0:1, :] = keys_t[i:i + 1, :]
        nsend[i, 1:2, :] = keys_t[8 + i:9 + i, :]
        nsend[i, 2:3, :] = jnp.broadcast_to(inverse, (1, 512))
    for i in range(1, 8):
        dy, core = i // 2, i % 2
        to = slot(0, (4 - dy) % 4, core)
        cp = remote(nsend.at[i], notes.at[to], nssem.at[i - 1], nrsem.at[to], dev(0, dy, flip=core == 1))
        cp.start()
        sends.append(cp)

    loads["t"].wait()
    loads["ws"].wait()
    base[...] = dot(tv[...], wsv[...])

    lanes = lax.broadcasted_iota(jnp.int32, (512, 512), 1).astype(F32)

    def gather_tile(t, init=False):
        pattern = jnp.where(koff[:, t:t + 1] == lanes, 1.0, 0.0).astype(BF16)
        added = dot(pattern, sbuf[t].reshape(512, 512))
        acc[...] = added if init else acc[...] + added

    sub = lax.broadcasted_iota(jnp.int32, (512, 512), 0).astype(F32)

    def link_tile(i):
        if i:
            remote(notes.at[i], notes.at[i], nssem.at[0], nrsem.at[i], dev(flip=True)).wait_recv()
        note = nsend if i == 0 else notes
        for col in range(2):
            links[i, col * 512:(col + 1) * 512, :] = jnp.where(note[i, col:col + 1, :] == sub, 1.0, 0.0).astype(BF16)
        scale[i:i + 1, :] = note[i, 2:3, :128]

    gather_tile(slot(0, 0, 0), True)
    link_tile(0)
    fetch(0, 3, 0)
    fetch(0, 1, 1)
    fetch(1, 0, 0)
    fetch(1, 0, 1)
    got_tile(0, 0)
    gather_tile(slot(0, 0, 1))
    fetch(0, 3, 1)
    fetch(0, 1, 0)
    fetch(1, 0, 2)
    fetch(1, 0, 3)
    gather_tile(slot(1, 0, 0))
    fetch(0, 3, 2)
    fetch(0, 1, 3)
    fetch(0, 2, 0)
    fetch(0, 2, 1)
    fetch(1, 3, 0)
    fetch(1, 1, 1)
    link_tile(1)
    link_tile(2)
    fetch(0, 1, 2)
    fetch(0, 3, 3)
    gather_tile(slot(0, 1, 0))
    fetch(1, 1, 0)
    fetch(1, 3, 1)
    gather_tile(slot(0, 3, 0))
    fetch(0, 2, 2)
    fetch(0, 2, 3)
    fetch(1, 3, 2)
    fetch(1, 1, 3)
    gather_tile(slot(0, 2, 0))
    fetch(1, 2, 0)
    fetch(1, 2, 1)
    got_tile(1, 0)
    gather_tile(slot(1, 0, 1))
    fetch(1, 1, 2)
    fetch(1, 3, 3)
    for dy in (1, 3, 2):
        got_tile(0, dy)
        gather_tile(slot(0, dy, 1))
    gather_tile(slot(1, 1, 0))
    gather_tile(slot(1, 3, 0))
    for i in range(3, 8):
        link_tile(i)
    fetch(1, 2, 2)
    fetch(1, 2, 3)
    for dy in (1, 3):
        got_tile(1, dy)
        gather_tile(slot(1, dy, 1))
    gather_tile(slot(1, 2, 0))
    got_tile(1, 2)
    gather_tile(slot(1, 2, 1))

    loads["wm"].wait()
    loads["cot"].wait()

    def ring(f, i, h, to_i, to, n):
        part = pl.ds(h * HALF, HALF)
        k = (f * 8 + to_i) * 2 + h
        cp = remote(gbuf.at[f, i, part], gbuf.at[f, to_i, part], ssend2.at[f * 14 + n], srecv2.at[k], to)
        cp.start()
        sends.append(cp)

    def arrive(f, i, h):
        part = pl.ds(h * HALF, HALF)
        remote(
            gbuf.at[f, i, part], gbuf.at[f, i, part], ssend2.at[0], srecv2.at[(f * 8 + i) * 2 + h], dev(flip=True)
        ).wait_recv()

    def own_out(f, h):
        outs = ((1, 0),) if h == 0 else ((3, 1), (3, 0), (1, 1))
        for dy, half in outs:
            ring(f, 0, half, (4 - dy) % 4 * 2, dev(0, dy), half * 2 + dy // 2)
        ring(f, 0, h, 1, dev(flip=True), 4 + h)

    def take(f, dy, h):
        arrive(f, dy * 2, h)
        if (dy, h) == (3, 0):
            ring(f, dy * 2, h, 4, dev(0, 1), 6)
        if (dy, h) == (1, 1):
            ring(f, dy * 2, h, 4, dev(0, 3), 7)
        ring(f, dy * 2, h, dy * 2 + 1, dev(flip=True), 8 + (dy - 1) * 2 + h)

    for h in range(2):
        part = pl.ds(h * HALF, HALF)
        mean = (acc[part, :] * inverse).astype(BF16)
        bbuf[part, :] = mean
        pre = base[part, :] + dot(mean, wmv[...])
        sig = jax.nn.sigmoid(pre)
        grad = (cotv[part, :].astype(F32) * sig * (1.0 + pre * (1.0 - sig))).astype(BF16)
        for f in range(PIECES):
            gbuf[f, 0, part, :] = grad[:, f * WIDE:(f + 1) * WIDE]
        own_out(0, h)
        acc[part, :] = pre * sig

    grads = jnp.concatenate([gbuf[f, 0] for f in range(PIECES)], axis=1)
    is_self = c == 0
    t_val, b_val = tv[...], bbuf[...]
    give[...] = dot(jnp.where(is_self, b_val, t_val), grads, 0, 0).astype(BF16)
    to_sib = remote(give, got, gsem.at[0], gsem.at[1], dev(flip=True))
    to_sib.start()
    sends.append(to_sib)
    base[...] = dot(jnp.where(is_self, t_val, b_val), grads, 0, 0)

    to_sib.wait_recv()
    wsend[...] = (base[...] + got[...].astype(F32)).astype(BF16).reshape(16, 32, 512)
    place = x * 4 + y
    for dx in range(1, XN):
        to_x = lax.rem(x + dx, XN)
        cp = remote(
            wsend.at[pl.ds(to_x * 4, 4)], wrecv.at[pl.ds(dx * 4 - 4, 4)], wssem.at[dx - 1], wrsem.at[dx - 1], dev(dx)
        )
        cp.start()
        sends.append(cp)

    def scatter(f, dy, core):
        i = dy * 2 + core
        added = dot(links[i], gbuf[f, i]) * scale[i:i + 1, :1]
        terms[f] = added if i == 0 else terms[f] + added

    def x_out(f):
        xsend[f] = terms[f].astype(BF16).reshape(2, 2, HALF, WIDE)
        for dx in range(1, XN):
            xh = lax.div(lax.rem(x + dx, XN), 2)
            cp = remote(
                xsend.at[f, dx % 2, xh], xrecv.at[f, dx - 1], xssem.at[f * 3 + dx - 1], xrsem.at[f * 3 + dx - 1], dev(dx)
            )
            cp.start()
            sends.append(cp)

    def z_out(f):
        total = xsend[f, 0, lax.div(x, 2)].astype(F32)
        for i in range(XN - 1):
            remote(
                xrecv.at[f, i], xrecv.at[f, i], xssem.at[0], xrsem.at[f * 3 + i], dev(flip=True)
            ).wait_recv()
            total = total + xrecv[f, i].astype(F32)
        dsend[f] = total.astype(BF16).reshape(8, 32, WIDE)
        for dz in range(1, ZN):
            n = f * 7 + dz - 1
            cp = remote(
                dsend.at[f, lax.rem(z + dz, ZN)], drecv.at[f, dz - 1], dssem.at[n], drsem.at[n], dev(dz=dz)
            )
            cp.start()
            sends.append(cp)

    def finish(f):
        total = dsend[f, z].astype(F32)
        for i in range(ZN - 1):
            remote(
                drecv.at[f, i], drecv.at[f, i], dssem.at[0], drsem.at[f * 7 + i], dev(flip=True)
            ).wait_recv()
            total = total + drecv[f, i].astype(F32)
        return dot(total.astype(BF16), wmv[:, f * WIDE:(f + 1) * WIDE], 1, 1)

    def weights_y():
        total = wsend[pl.ds(x * 4, 4)].astype(F32)
        for i in range(XN - 1):
            got_x = wrecv.at[pl.ds(i * 4, 4)]
            remote(got_x, got_x, wssem.at[0], wrsem.at[i], dev(flip=True)).wait_recv()
            total = total + got_x[...].astype(F32)
        ysend[...] = total.astype(BF16)
        for dy in range(1, YN):
            cp = remote(
                ysend.at[lax.rem(y + dy, YN)], yrecv.at[dy - 1], wssem.at[2 + dy], wrsem.at[2 + dy], dev(0, dy)
            )
            cp.start()
            sends.append(cp)

    def weights_z():
        total = ysend[y].astype(F32)
        for i in range(YN - 1):
            remote(yrecv.at[i], yrecv.at[i], wssem.at[0], wrsem.at[3 + i], dev(flip=True)).wait_recv()
            total = total + yrecv[i].astype(F32)
        zbuf[z] = total.astype(BF16)
        for dz in range(1, ZN):
            cp = remote(zbuf.at[z], zbuf.at[z], zssem.at[dz], zrsem.at[z], dev(0, 0, dz))
            cp.start()
            sends.append(cp)

    def weights_out():
        for dz in range(1, ZN):
            peer = lax.rem(z + dz, ZN)
            remote(zbuf.at[peer], zbuf.at[peer], zssem.at[dz], zrsem.at[peer], dev(flip=True)).wait_recv()
        total = zbuf[0].astype(F32)
        for i in range(1, ZN):
            total = total + zbuf[i].astype(F32)
        wres[c, place] = total.astype(BF16)
        for i, (dx, dy) in enumerate(plane):
            cp = remote(wres.at[c, place], wres.at[c, place], assem.at[i], arsem.at[i], dev(dx, dy))
            cp.start()
            sends.append(cp)

    def sibling(f, dy):
        for h in range(2):
            arrive(f, dy * 2 + 1, h)
        scatter(f, dy, 1)

    old = list(sends)
    sends.clear()
    take(0, 3, 0)
    take(0, 1, 1)
    tgv[...] = (cotv[...].astype(F32) + dot(grads, wsv[...], 1, 1)).astype(BF16)
    take(0, 3, 1)
    take(0, 1, 0)
    own_out(1, 0)
    own_out(1, 1)
    scatter(0, 0, 0)
    sibling(0, 0)
    scatter(0, 3, 0)
    scatter(0, 1, 0)
    take(0, 2, 0)
    take(0, 2, 1)
    sibling(0, 3)
    sibling(0, 1)
    weights_y()
    scatter(0, 2, 0)
    sibling(0, 2)
    x_out(0)
    take(1, 3, 0)
    take(1, 1, 1)
    scatter(1, 0, 0)
    sibling(1, 0)
    weights_z()
    take(1, 3, 1)
    take(1, 1, 0)
    scatter(1, 3, 0)
    scatter(1, 1, 0)
    take(1, 2, 0)
    take(1, 2, 1)
    sibling(1, 3)
    sibling(1, 1)
    scatter(1, 2, 0)
    sibling(1, 2)
    x_out(1)
    for cp in old:
        cp.wait_send()
    updv[...] = (tv[...].astype(F32) + acc[...]).astype(BF16)
    z_out(0)
    weights_out()
    out = finish(0)
    z_out(1)
    settle()

    for dx in (0, 1, 3, 2):
        for dy in range(YN):
            if (dx, dy) != (0, 0):
                i = plane.index((dx, dy))
                peer = lax.rem(x + (XN - dx), XN) * 4 + lax.rem(y + (YN - dy), YN)
                remote(wres.at[c, peer], wres.at[c, peer], assem.at[i], arsem.at[i], dev(flip=True)).wait_recv()
        part = wres.at[c, pl.ds(lax.rem(x + (XN - dx), XN) * 4, 4)]
        cp = remote(part, part, bssem.at[dx], brsem.at[dx], dev(flip=True))
        cp.start()
        sends.append(cp)

    sg_ref[...] = (out + finish(1)).astype(BF16)

    def self_done():
        self_ref[...] = wres[0].reshape(512, 512).astype(F32) * 131072 ** (-0.5)

    def message_done():
        message_ref[...] = wres[1].reshape(512, 512).astype(F32) * 8192 ** (-0.5)

    pl.when(c == 0)(self_done)
    pl.when(c == 1)(message_done)
    for dx in range(XN):
        part = wres.at[1 - c, pl.ds(lax.rem(x + (XN - dx), XN) * 4, 4)]
        remote(part, part, bssem.at[dx], brsem.at[dx], dev(flip=True)).wait_recv()
    pl.when(c == 1)(self_done)
    pl.when(c == 0)(message_done)
    settle()


def place_outputs(*refs):
    count = len(refs) // 2
    copies = [pltpu.make_async_copy(refs[i], refs[count + i], refs[-1].at[i]) for i in range(count)]
    for cp in copies:
        cp.start()
    for cp in copies:
        cp.wait()


def local(
    source_table, target_table, message_weight, self_weight, tile_lists, key_offsets, list_lengths, cotangent
):
    any_spec = pl.BlockSpec(memory_space=pl.ANY)
    vmem = pl.BlockSpec(memory_space=pltpu.VMEM)
    dma = pltpu.SemaphoreType.DMA
    square = (512, 512)
    shapes = ((square, BF16), (square, BF16), ((32, 512), BF16), (square, F32), (square, F32))
    held = pl.pallas_call(
        kernel,
        out_shape=tuple(pltpu.VMEM(*shape) for shape in shapes),
        in_specs=[any_spec, any_spec, any_spec, any_spec, vmem, vmem, vmem, any_spec],
        out_specs=(vmem,) * 5,
        scratch_shapes=[
            pltpu.VMEM((16, 4, 128, 512), BF16),
            pltpu.VMEM((PIECES, 8, 512, WIDE), BF16),
            pltpu.VMEM((8, 8, 512), F32),
            pltpu.VMEM((8, 8, 512), F32),
            pltpu.VMEM((8, 1024, 512), BF16),
            pltpu.VMEM((8, 128), F32),
            pltpu.VMEM(square, BF16),
            pltpu.VMEM(square, BF16),
            pltpu.VMEM(square, BF16),
            pltpu.VMEM(square, BF16),
            pltpu.VMEM(square, F32),
            pltpu.VMEM(square, F32),
            pltpu.VMEM(square, BF16),
            pltpu.VMEM((512, 16), F32),
            pltpu.VMEM((PIECES, 1024, WIDE), F32),
            pltpu.VMEM(square, BF16),
            pltpu.VMEM(square, BF16),
            pltpu.VMEM((16, 32, 512), BF16),
            pltpu.VMEM((12, 32, 512), BF16),
            pltpu.VMEM((4, 32, 512), BF16),
            pltpu.VMEM((3, 32, 512), BF16),
            pltpu.VMEM((8, 32, 512), BF16),
            pltpu.VMEM((2, 16, 32, 512), BF16),
            pltpu.VMEM((PIECES, 2, 2, HALF, WIDE), BF16),
            pltpu.VMEM((PIECES, 3, HALF, WIDE), BF16),
            pltpu.VMEM((PIECES, 8, 32, WIDE), BF16),
            pltpu.VMEM((PIECES, 7, 32, WIDE), BF16),
            dma((5,)),
            dma((44,)), dma((64,)),
            dma((7,)), dma((8,)),
            dma((14 * PIECES,)), dma((16 * PIECES,)),
            dma((2,)),
            dma((6,)), dma((6,)),
            dma((8,)), dma((8,)),
            dma((15,)), dma((15,)),
            dma((4,)), dma((4,)),
            dma((3 * PIECES,)), dma((3 * PIECES,)),
            dma((7 * PIECES,)), dma((7 * PIECES,)),
            pltpu.SemaphoreType.REGULAR, pltpu.SemaphoreType.REGULAR,
        ],
        compiler_params=pltpu.CompilerParams(
            collective_id=0, has_side_effects=True, vmem_limit_bytes=56 * 1024 * 1024
        ),
    )(
        source_table.reshape(4, 128, 512), target_table, message_weight, self_weight, tile_lists, key_offsets.T,
        list_lengths.reshape(1, 1), cotangent,
    )
    return pl.pallas_call(
        place_outputs,
        out_shape=tuple(jax.ShapeDtypeStruct(*shape) for shape in shapes),
        in_specs=[vmem] * 5,
        out_specs=(any_spec,) * 5,
        scratch_shapes=[dma((5,))],
    )(*[pltpu.with_memory_space_constraint(one, pltpu.VMEM) for one in held])


def solution(mesh):
    placed = (
        P("blk", None),
        P(("row", "blk"), None),
        P(),
        P(),
        P(("row", "blk"), None),
        P(("row", "blk"), None),
        P(("row", "blk")),
        P(("row", "blk"), None),
    )
    return jax.shard_map(
        local,
        mesh=mesh,
        in_specs=placed,
        out_specs=(
            P(("row", "blk"), None),
            P(("row", "blk"), None),
            P(("blk", "row"), None),
            P(),
            P(),
        ),
        check_vma=False,
    )
```

```python
import functools

import jax
import jax.numpy as jnp
from jax import lax
from jax.experimental import pallas as pl
from jax.experimental.pallas import tpu as pltpu
from jax.sharding import PartitionSpec as P

XN, YN, ZN = 4, 4, 8
HALF = 256
PIECES = 2
WIDE = 512 // PIECES
F32 = jnp.float32
BF16 = jnp.bfloat16


def dot(a, b, ca=1, cb=0):
    return lax.dot_general(a, b, (((ca,), (cb,)), ((), ())), preferred_element_type=F32)


def slot(col, dy, core):
    return col * 8 + dy * 2 + core


def kernel(
    s_hbm, t_hbm, wm_hbm, ws_hbm, lists_ref, ko_ref, len_ref, cot_hbm,
    updv, tgv, sg_ref, self_ref, message_ref,
    sbuf, gbuf, nsend, notes, links, scale, tv, cotv, wmv, wsv, acc, base, bbuf, koff, terms,
    give, got, wsend, wrecv, ysend, yrecv, zbuf, wres, xsend, xrecv, dsend, drecv,
    lsem, ssend1, srecv1, nssem, nrsem, ssend2, srecv2, gsem, wssem, wrsem, zssem, zrsem, assem, arsem, bssem, brsem,
    xssem, xrsem, dssem, drsem, near_sem, far_sem,
):
    r = lax.axis_index("row")
    b = lax.axis_index("blk")
    x = lax.div(r, 8) * 2 + lax.div(b, 8)
    y = lax.rem(lax.div(b, 2), 4)
    z = lax.rem(r, 8)
    c = lax.rem(b, 2)

    def dev(dx=0, dy=0, dz=0, flip=False):
        xx = lax.rem(x + dx, XN)
        yy = lax.rem(y + dy, YN)
        zz = lax.rem(z + dz, ZN)
        cc = 1 - c if flip else c
        return {"row": lax.div(xx, 2) * 8 + zz, "blk": lax.rem(xx, 2) * 8 + yy * 2 + cc}

    def remote(src, dst, ss, rs, to):
        return pltpu.make_async_remote_copy(
            src_ref=src, dst_ref=dst, send_sem=ss, recv_sem=rs,
            device_id=to, device_id_type=pl.DeviceIdType.MESH,
        )

    loads = {}
    for i, (name, src, dst) in enumerate((
        ("s", s_hbm, sbuf.at[0]), ("t", t_hbm, tv), ("ws", ws_hbm, wsv), ("wm", wm_hbm, wmv), ("cot", cot_hbm, cotv),
    )):
        loads[name] = pltpu.make_async_copy(src, dst, lsem.at[i])
        loads[name].start()

    plane = [(dx, dy) for dx in range(XN) for dy in range(YN) if (dx, dy) != (0, 0)]
    nearest = [dev(flip=True), dev(1), dev(3), dev(0, 1), dev(0, 3), dev(dz=1), dev(dz=ZN - 1)]

    second = [dev(2), dev(0, 2), dev(dz=2), dev(dz=ZN - 2)]

    def greet(sem, others):
        for to in others:
            pl.semaphore_signal(sem, inc=1, device_id=to, device_id_type=pl.DeviceIdType.MESH)

    barrier = pltpu.get_barrier_semaphore()
    greet(barrier, nearest)
    pl.semaphore_wait(barrier, len(nearest))

    sends = []

    def settle():
        for cp in sends:
            cp.wait_send()
        sends.clear()


    parity = lax.rem(z, 2)
    made = [0]

    def part_of(t, role):
        base_row = 2 * parity if role < 2 else 2 - 2 * parity
        return sbuf.at[t, base_row + role % 2]

    def push(t, role, to_t, to_role, to):
        cp = remote(part_of(t, role), part_of(to_t, role), ssend1.at[made[0]], srecv1.at[to_t * 4 + to_role], to)
        cp.start()
        made[0] += 1
        sends.append(cp)

    def got_part(col, dy, core, role):
        t = slot(col, dy, core)
        remote(part_of(t, role), part_of(t, role), ssend1.at[0], srecv1.at[t * 4 + role], dev(flip=True)).wait_recv()

    def half_of(t, pair):
        return sbuf.at[t, pl.ds(2 * parity if pair == 0 else 2 - 2 * parity, 2)]

    def push_half(t, to_t, pair):
        half = half_of(t, pair)
        cp = remote(half, half_of(to_t, pair), ssend1.at[made[0]], srecv1.at[to_t * 4 + 2 * pair], dev(flip=True))
        cp.start()
        made[0] += 1
        sends.append(cp)

    def got_tile(col, dy):
        t = slot(col, dy, 1)
        for pair in range(2):
            half = half_of(t, pair)
            remote(half, half, ssend1.at[0], srecv1.at[t * 4 + 2 * pair], dev(flip=True)).wait_recv()

    here = set()

    def fetch(col, dy, role):
        got_part(col, dy, 0, role)
        t = slot(col, dy, 0)
        if col == 0 and dy == 3 and role in (0, 2):
            push(t, role, slot(0, 2, 0), role, dev(0, 1))
        if col == 0 and dy == 1 and role in (1, 3):
            push(t, role, slot(0, 2, 0), role, dev(0, 3))
        if role < 2 and (col, dy) not in ((0, 2), (1, 0)):
            push(t, role, t, role + 2, dev(dz=ZN - 1 if role == 0 else 1))
        if role < 2 and col == 0:
            push(t, role, slot(1, dy, 0), role, dev(1 if role == 0 else 3))
        here.add((t, role))
        if (t, role ^ 1) in here:
            push_half(t, slot(col, dy, 1), role // 2)

    loads["s"].wait()
    for role in (0, 1):
        push(0, role, slot(0, 3, 0), role, dev(0, 1))
        push(0, 1 - role, slot(0, 1, 0), 1 - role, dev(0, 3))
        push(0, 2 * role, slot(1, 0, 0), 2 * role, dev(1))
        push(0, 2 * role + 1, slot(1, 0, 0), 2 * role + 1, dev(3))
    for pair in range(2):
        push_half(0, slot(0, 0, 1), pair)

    k_row = lax.broadcasted_iota(jnp.int32, (16, 16), 0)
    s_col = lax.broadcasted_iota(jnp.int32, (16, 16), 1)
    kc, kd, ke = k_row // 8, (k_row // 2) % 4, k_row % 2
    xl = lax.rem(x, 2)
    tile_id = ((xl + kc) % 2) * 8 + ((y + kd) % 4) * 2 + (c + ke) % 2
    pick = ((lists_ref[...] == tile_id) & (s_col < len_ref[...])).astype(F32).astype(BF16)
    keys = ko_ref[...] + 1
    k_hi = (keys // 256).astype(F32).astype(BF16)
    k_lo = (keys % 256).astype(F32).astype(BF16)
    koff[...] = dot(k_hi, pick, 0, 1) * 256.0 + dot(k_lo, pick, 0, 1) - 1.0
    length = len_ref[...].astype(F32)
    inverse = 1.0 / length
    greet(near_sem, nearest)

    lanes = lax.broadcasted_iota(jnp.int32, (512, 512), 1).astype(F32)

    def gather_tile(t, init=False):
        pattern = jnp.where(koff[:, t:t + 1] == lanes, 1.0, 0.0).astype(BF16)
        added = dot(pattern, sbuf[t].reshape(512, 512))
        acc[...] = added if init else acc[...] + added

    sub = lax.broadcasted_iota(jnp.int32, (512, 512), 0).astype(F32)

    def link_tile(i):
        if i:
            remote(notes.at[i], notes.at[i], nssem.at[0], nrsem.at[i], dev(flip=True)).wait_recv()
        note = nsend if i == 0 else notes
        for col in range(2):
            links[i, col * 512:(col + 1) * 512, :] = jnp.where(note[i, col:col + 1, :] == sub, 1.0, 0.0).astype(BF16)
        scale[i:i + 1, :] = note[i, 2:3, :128]

    gather_tile(slot(0, 0, 0), True)
    fetch(0, 3, 0)
    fetch(0, 1, 1)
    fetch(1, 0, 0)
    fetch(1, 0, 1)
    pl.semaphore_wait(near_sem, len(nearest))
    greet(far_sem, second)
    got_tile(0, 0)
    gather_tile(slot(0, 0, 1))
    fetch(0, 3, 1)
    fetch(0, 1, 0)
    fetch(1, 0, 2)
    fetch(1, 0, 3)
    pl.semaphore_wait(far_sem, len(second))
    keys_t = dot(pick, k_hi) * 256.0 + dot(pick, k_lo) - 1.0
    for i in range(8):
        nsend[i, 0:1, :] = keys_t[i:i + 1, :]
        nsend[i, 1:2, :] = keys_t[8 + i:9 + i, :]
        nsend[i, 2:3, :] = jnp.broadcast_to(inverse, (1, 512))
    for i in range(1, 8):
        dy, core = i // 2, i % 2
        to = slot(0, (4 - dy) % 4, core)
        cp = remote(nsend.at[i], notes.at[to], nssem.at[i - 1], nrsem.at[to], dev(0, dy, flip=core == 1))
        cp.start()
        sends.append(cp)

    fetch(0, 3, 2)
    fetch(0, 1, 3)
    fetch(0, 2, 0)
    fetch(0, 2, 1)
    fetch(1, 3, 0)
    fetch(1, 1, 1)
    gather_tile(slot(1, 0, 0))
    loads["t"].wait()
    loads["ws"].wait()
    base[...] = dot(tv[...], wsv[...])

    fetch(0, 1, 2)
    fetch(0, 3, 3)
    gather_tile(slot(0, 1, 0))
    fetch(1, 1, 0)
    fetch(1, 3, 1)
    gather_tile(slot(0, 3, 0))
    fetch(0, 2, 2)
    fetch(0, 2, 3)
    fetch(1, 3, 2)
    fetch(1, 1, 3)
    gather_tile(slot(0, 2, 0))
    fetch(1, 2, 0)
    fetch(1, 2, 1)
    got_tile(1, 0)
    gather_tile(slot(1, 0, 1))
    link_tile(0)
    link_tile(1)
    fetch(1, 1, 2)
    fetch(1, 3, 3)
    for dy in (1, 3, 2):
        got_tile(0, dy)
        gather_tile(slot(0, dy, 1))
    gather_tile(slot(1, 1, 0))
    gather_tile(slot(1, 3, 0))
    for i in range(2, 8):
        link_tile(i)
    fetch(1, 2, 2)
    fetch(1, 2, 3)
    for dy in (1, 3):
        got_tile(1, dy)
        gather_tile(slot(1, dy, 1))
    gather_tile(slot(1, 2, 0))
    got_tile(1, 2)
    gather_tile(slot(1, 2, 1))

    loads["wm"].wait()
    loads["cot"].wait()

    def ring(f, i, h, to_i, to, n):
        part = pl.ds(h * HALF, HALF)
        k = (f * 8 + to_i) * 2 + h
        cp = remote(gbuf.at[f, i, part], gbuf.at[f, to_i, part], ssend2.at[f * 14 + n], srecv2.at[k], to)
        cp.start()
        sends.append(cp)

    def arrive(f, i, h):
        part = pl.ds(h * HALF, HALF)
        remote(
            gbuf.at[f, i, part], gbuf.at[f, i, part], ssend2.at[0], srecv2.at[(f * 8 + i) * 2 + h], dev(flip=True)
        ).wait_recv()

    def own_out(f, h):
        outs = ((1, 0),) if h == 0 else ((3, 1), (3, 0), (1, 1))
        for dy, half in outs:
            ring(f, 0, half, (4 - dy) % 4 * 2, dev(0, dy), half * 2 + dy // 2)
        ring(f, 0, h, 1, dev(flip=True), 4 + h)

    def take(f, dy, h):
        arrive(f, dy * 2, h)
        if (dy, h) == (3, 0):
            ring(f, dy * 2, h, 4, dev(0, 1), 6)
        if (dy, h) == (1, 1):
            ring(f, dy * 2, h, 4, dev(0, 3), 7)
        ring(f, dy * 2, h, dy * 2 + 1, dev(flip=True), 8 + (dy - 1) * 2 + h)

    for h in range(2):
        part = pl.ds(h * HALF, HALF)
        mean = (acc[part, :] * inverse).astype(BF16)
        bbuf[part, :] = mean
        pre = base[part, :] + dot(mean, wmv[...])
        sig = jax.nn.sigmoid(pre)
        grad = (cotv[part, :].astype(F32) * sig * (1.0 + pre * (1.0 - sig))).astype(BF16)
        for f in range(PIECES):
            gbuf[f, 0, part, :] = grad[:, f * WIDE:(f + 1) * WIDE]
        own_out(0, h)
        acc[part, :] = pre * sig

    grads = jnp.concatenate([gbuf[f, 0] for f in range(PIECES)], axis=1)
    is_self = c == 0
    t_val, b_val = tv[...], bbuf[...]
    give[...] = dot(jnp.where(is_self, b_val, t_val), grads, 0, 0).astype(BF16)
    to_sib = remote(give, got, gsem.at[0], gsem.at[1], dev(flip=True))
    to_sib.start()
    sends.append(to_sib)
    base[...] = dot(jnp.where(is_self, t_val, b_val), grads, 0, 0)

    to_sib.wait_recv()
    wsend[...] = (base[...] + got[...].astype(F32)).astype(BF16).reshape(16, 32, 512)
    place = x * 4 + y
    for dx in range(1, XN):
        to_x = lax.rem(x + dx, XN)
        cp = remote(
            wsend.at[pl.ds(to_x * 4, 4)], wrecv.at[pl.ds(dx * 4 - 4, 4)], wssem.at[dx - 1], wrsem.at[dx - 1], dev(dx)
        )
        cp.start()
        sends.append(cp)

    def scatter(f, dy, core):
        i = dy * 2 + core
        added = dot(links[i], gbuf[f, i]) * scale[i:i + 1, :1]
        terms[f] = added if i == 0 else terms[f] + added

    def x_out(f):
        xsend[f] = terms[f].astype(BF16).reshape(2, 2, HALF, WIDE)
        for dx in range(1, XN):
            xh = lax.div(lax.rem(x + dx, XN), 2)
            cp = remote(
                xsend.at[f, dx % 2, xh], xrecv.at[f, dx - 1], xssem.at[f * 3 + dx - 1], xrsem.at[f * 3 + dx - 1], dev(dx)
            )
            cp.start()
            sends.append(cp)

    def z_out(f):
        total = xsend[f, 0, lax.div(x, 2)].astype(F32)
        for i in range(XN - 1):
            remote(
                xrecv.at[f, i], xrecv.at[f, i], xssem.at[0], xrsem.at[f * 3 + i], dev(flip=True)
            ).wait_recv()
            total = total + xrecv[f, i].astype(F32)
        dsend[f] = total.astype(BF16).reshape(8, 32, WIDE)
        for dz in range(1, ZN):
            n = f * 7 + dz - 1
            cp = remote(
                dsend.at[f, lax.rem(z + dz, ZN)], drecv.at[f, dz - 1], dssem.at[n], drsem.at[n], dev(dz=dz)
            )
            cp.start()
            sends.append(cp)

    def finish(f):
        total = dsend[f, z].astype(F32)
        for i in range(ZN - 1):
            remote(
                drecv.at[f, i], drecv.at[f, i], dssem.at[0], drsem.at[f * 7 + i], dev(flip=True)
            ).wait_recv()
            total = total + drecv[f, i].astype(F32)
        return dot(total.astype(BF16), wmv[:, f * WIDE:(f + 1) * WIDE], 1, 1)

    def weights_y():
        total = wsend[pl.ds(x * 4, 4)].astype(F32)
        for i in range(XN - 1):
            got_x = wrecv.at[pl.ds(i * 4, 4)]
            remote(got_x, got_x, wssem.at[0], wrsem.at[i], dev(flip=True)).wait_recv()
            total = total + got_x[...].astype(F32)
        ysend[...] = total.astype(BF16)
        for dy in range(1, YN):
            cp = remote(
                ysend.at[lax.rem(y + dy, YN)], yrecv.at[dy - 1], wssem.at[2 + dy], wrsem.at[2 + dy], dev(0, dy)
            )
            cp.start()
            sends.append(cp)

    def weights_z():
        total = ysend[y].astype(F32)
        for i in range(YN - 1):
            remote(yrecv.at[i], yrecv.at[i], wssem.at[0], wrsem.at[3 + i], dev(flip=True)).wait_recv()
            total = total + yrecv[i].astype(F32)
        zbuf[z] = total.astype(BF16)
        for dz in range(1, ZN):
            cp = remote(zbuf.at[z], zbuf.at[z], zssem.at[dz], zrsem.at[z], dev(0, 0, dz))
            cp.start()
            sends.append(cp)

    def weights_out():
        for dz in range(1, ZN):
            peer = lax.rem(z + dz, ZN)
            remote(zbuf.at[peer], zbuf.at[peer], zssem.at[dz], zrsem.at[peer], dev(flip=True)).wait_recv()
        total = zbuf[0].astype(F32)
        for i in range(1, ZN):
            total = total + zbuf[i].astype(F32)
        wres[c, place] = total.astype(BF16)
        for i, (dx, dy) in enumerate(plane):
            cp = remote(wres.at[c, place], wres.at[c, place], assem.at[i], arsem.at[i], dev(dx, dy))
            cp.start()
            sends.append(cp)

    def sibling(f, dy):
        for h in range(2):
            arrive(f, dy * 2 + 1, h)
        scatter(f, dy, 1)

    old = list(sends)
    sends.clear()
    take(0, 3, 0)
    take(0, 1, 1)
    tgv[...] = (cotv[...].astype(F32) + dot(grads, wsv[...], 1, 1)).astype(BF16)
    take(0, 3, 1)
    take(0, 1, 0)
    own_out(1, 0)
    own_out(1, 1)
    scatter(0, 0, 0)
    sibling(0, 0)
    scatter(0, 3, 0)
    scatter(0, 1, 0)
    take(0, 2, 0)
    take(0, 2, 1)
    sibling(0, 3)
    sibling(0, 1)
    scatter(0, 2, 0)
    sibling(0, 2)
    x_out(0)
    weights_y()
    take(1, 3, 0)
    take(1, 1, 1)
    scatter(1, 0, 0)
    sibling(1, 0)
    weights_z()
    take(1, 3, 1)
    take(1, 1, 0)
    scatter(1, 3, 0)
    scatter(1, 1, 0)
    take(1, 2, 0)
    take(1, 2, 1)
    sibling(1, 3)
    sibling(1, 1)
    scatter(1, 2, 0)
    sibling(1, 2)
    x_out(1)
    for cp in old:
        cp.wait_send()
    updv[...] = (tv[...].astype(F32) + acc[...]).astype(BF16)
    z_out(0)
    weights_out()
    z_out(1)
    out = finish(0)
    settle()

    for dx in (0, 1, 3, 2):
        for dy in range(YN):
            if (dx, dy) != (0, 0):
                i = plane.index((dx, dy))
                peer = lax.rem(x + (XN - dx), XN) * 4 + lax.rem(y + (YN - dy), YN)
                remote(wres.at[c, peer], wres.at[c, peer], assem.at[i], arsem.at[i], dev(flip=True)).wait_recv()
        part = wres.at[c, pl.ds(lax.rem(x + (XN - dx), XN) * 4, 4)]
        cp = remote(part, part, bssem.at[dx], brsem.at[dx], dev(flip=True))
        cp.start()
        sends.append(cp)

    sg_ref[...] = (out + finish(1)).astype(BF16)

    def self_done():
        self_ref[...] = wres[0].reshape(512, 512).astype(F32) * 131072 ** (-0.5)

    def message_done():
        message_ref[...] = wres[1].reshape(512, 512).astype(F32) * 8192 ** (-0.5)

    pl.when(c == 0)(self_done)
    pl.when(c == 1)(message_done)
    for dx in range(XN):
        part = wres.at[1 - c, pl.ds(lax.rem(x + (XN - dx), XN) * 4, 4)]
        remote(part, part, bssem.at[dx], brsem.at[dx], dev(flip=True)).wait_recv()
    pl.when(c == 1)(self_done)
    pl.when(c == 0)(message_done)
    settle()


def place_outputs(*refs):
    count = len(refs) // 2
    copies = [pltpu.make_async_copy(refs[i], refs[count + i], refs[-1].at[i]) for i in range(count)]
    for cp in copies:
        cp.start()
    for cp in copies:
        cp.wait()


def local(
    source_table, target_table, message_weight, self_weight, tile_lists, key_offsets, list_lengths, cotangent
):
    any_spec = pl.BlockSpec(memory_space=pl.ANY)
    vmem = pl.BlockSpec(memory_space=pltpu.VMEM)
    dma = pltpu.SemaphoreType.DMA
    square = (512, 512)
    shapes = ((square, BF16), (square, BF16), ((32, 512), BF16), (square, F32), (square, F32))
    held = pl.pallas_call(
        kernel,
        out_shape=tuple(pltpu.VMEM(*shape) for shape in shapes),
        in_specs=[any_spec, any_spec, any_spec, any_spec, vmem, vmem, vmem, any_spec],
        out_specs=(vmem,) * 5,
        scratch_shapes=[
            pltpu.VMEM((16, 4, 128, 512), BF16),
            pltpu.VMEM((PIECES, 8, 512, WIDE), BF16),
            pltpu.VMEM((8, 8, 512), F32),
            pltpu.VMEM((8, 8, 512), F32),
            pltpu.VMEM((8, 1024, 512), BF16),
            pltpu.VMEM((8, 128), F32),
            pltpu.VMEM(square, BF16),
            pltpu.VMEM(square, BF16),
            pltpu.VMEM(square, BF16),
            pltpu.VMEM(square, BF16),
            pltpu.VMEM(square, F32),
            pltpu.VMEM(square, F32),
            pltpu.VMEM(square, BF16),
            pltpu.VMEM((512, 16), F32),
            pltpu.VMEM((PIECES, 1024, WIDE), F32),
            pltpu.VMEM(square, BF16),
            pltpu.VMEM(square, BF16),
            pltpu.VMEM((16, 32, 512), BF16),
            pltpu.VMEM((12, 32, 512), BF16),
            pltpu.VMEM((4, 32, 512), BF16),
            pltpu.VMEM((3, 32, 512), BF16),
            pltpu.VMEM((8, 32, 512), BF16),
            pltpu.VMEM((2, 16, 32, 512), BF16),
            pltpu.VMEM((PIECES, 2, 2, HALF, WIDE), BF16),
            pltpu.VMEM((PIECES, 3, HALF, WIDE), BF16),
            pltpu.VMEM((PIECES, 8, 32, WIDE), BF16),
            pltpu.VMEM((PIECES, 7, 32, WIDE), BF16),
            dma((5,)),
            dma((44,)), dma((64,)),
            dma((7,)), dma((8,)),
            dma((14 * PIECES,)), dma((16 * PIECES,)),
            dma((2,)),
            dma((6,)), dma((6,)),
            dma((8,)), dma((8,)),
            dma((15,)), dma((15,)),
            dma((4,)), dma((4,)),
            dma((3 * PIECES,)), dma((3 * PIECES,)),
            dma((7 * PIECES,)), dma((7 * PIECES,)),
            pltpu.SemaphoreType.REGULAR, pltpu.SemaphoreType.REGULAR,
        ],
        compiler_params=pltpu.CompilerParams(
            collective_id=0, has_side_effects=True, vmem_limit_bytes=56 * 1024 * 1024
        ),
    )(
        source_table.reshape(4, 128, 512), target_table, message_weight, self_weight, tile_lists, key_offsets.T,
        list_lengths.reshape(1, 1), cotangent,
    )
    return pl.pallas_call(
        place_outputs,
        out_shape=tuple(jax.ShapeDtypeStruct(*shape) for shape in shapes),
        in_specs=[vmem] * 5,
        out_specs=(any_spec,) * 5,
        scratch_shapes=[dma((5,))],
    )(*[pltpu.with_memory_space_constraint(one, pltpu.VMEM) for one in held])


def solution(mesh):
    placed = (
        P("blk", None),
        P(("row", "blk"), None),
        P(),
        P(),
        P(("row", "blk"), None),
        P(("row", "blk"), None),
        P(("row", "blk")),
        P(("row", "blk"), None),
    )
    return jax.shard_map(
        local,
        mesh=mesh,
        in_specs=placed,
        out_specs=(
            P(("row", "blk"), None),
            P(("row", "blk"), None),
            P(("blk", "row"), None),
            P(),
            P(),
        ),
        check_vma=False,
    )
```
